512 devices in a mesh: member: 16 (over x, y_lo), space: 16 (over z, core), dp: 2 (over y_hi).
Axes of the slice: x: 4, y: 8 (y_hi: 2, y_lo: 4; y = y_hi * 4 + y_lo), z: 8, core: 2. Of those that a mesh axis runs over, the one named last changes fastest.
Arguments:
- latent: bfloat16 [16, 2, 16384, 1024], P('member', 'dp', 'space'), may hold values from -6 to 6
- target: bfloat16 [2, 100, 16384], P('dp', None, 'space'), may hold values from -6 to 6
- weight: bfloat16 [100, 1024], replicated, may hold values from -0.1875 to 0.1875
- bias: float32 [100], replicated, may hold values from -3 to 3
- gain: float32 [1024], replicated, may hold values from 0.1 to 1.9
- channel_weight: float32 [100], replicated, may hold values from 0.25 to 4
- band_offsets: int32 [17], replicated, may hold values from 0 to 80, as said below
- row_points: int32 [128], replicated, may hold values from 64 to 128, as said below
Outputs:
- grad_latent: bfloat16 [16, 2, 16384, 1024], P('member', 'dp', 'space')
- grad_weight: float32 [100, 1024], replicated
- grad_bias: float32 [100], replicated
- grad_gain: float32 [1024], replicated
- loss: float32 [], replicated
The draws below stay inside these ranges and needn't reach their ends.
Inputs may be any that keep to these rules, and one draw needn't show every extreme that they name: `band_offsets`: nondecreasing, starting at 0; band s holds rows band_offsets[s] to band_offsets[s+1] - 1, at least 2 and at most 8 rows, and its points fill its first slots. `row_points`: the rows of one band hold at most 1024 points together, exactly 1024 in some band.
All inputs are finite; a program needn't handle non-finite values.
Results may differ from the reference program's by a relative error of at most 0.0084.
Values sent between devices are 32-bit elements; how exact they have to be, the bound alone decides.
A program may use at most 64 MiB of HBM per device.

```python
import math
import jax
import jax.numpy as jnp
from jax import lax

H = 1024
C = 100
BAND_ROWS = 8
ROW_PTS = 128
PTS_DEV = 1024
POINTS = 16384
LAT_ROWS = 128
BATCH = 2
MEMBERS = 16
N_SPACE = 16


def band_layout(key):
    inner = jax.random.fold_in(key, 7)
    key_rows, key_points, key_full = jax.random.split(inner, 3)
    fewest = max(1, BAND_ROWS // 3)
    pair_count = N_SPACE // 2
    pair_rows = jax.random.randint(key_rows, (pair_count,), fewest, BAND_ROWS + 1, dtype=jnp.int32)
    full_band = jax.random.randint(key_full, (), 0, N_SPACE, dtype=jnp.int32)
    full_pair = full_band // 2
    forced = jnp.where(full_band % 2 == 0, BAND_ROWS, fewest).astype(jnp.int32)
    pair_rows = jnp.where(jnp.arange(pair_count, dtype=jnp.int32) == full_pair, forced, pair_rows).astype(jnp.int32)
    partner_rows = (BAND_ROWS + fewest - pair_rows).astype(jnp.int32)
    band_rows = jnp.stack([pair_rows, partner_rows], axis=1).reshape(N_SPACE).astype(jnp.int32)
    offsets = jnp.concatenate([jnp.zeros((1,), jnp.int32), jnp.cumsum(band_rows).astype(jnp.int32)])
    points = jax.random.randint(key_points, (N_SPACE * BAND_ROWS,), ROW_PTS // 2, ROW_PTS + 1, dtype=jnp.int32)
    row_ids = jnp.arange(N_SPACE * BAND_ROWS, dtype=jnp.int32)
    start_row = jnp.sum(jnp.where(jnp.arange(N_SPACE + 1, dtype=jnp.int32) == full_band, offsets, 0))
    in_full = (row_ids >= start_row) & (row_ids < start_row + BAND_ROWS)
    points = jnp.where(in_full, ROW_PTS, points).astype(jnp.int32)
    return (offsets, points)


def draw_band_offsets(key, part):
    return band_layout(key)[0]


def draw_row_points(key, part):
    return band_layout(key)[1]


def levels(rng, dims, cuts, least, top_value):
    factor_of = 1.0
    for position, blocks in cuts:
        steps = jax.random.uniform(jax.random.fold_in(jax.random.fold_in(rng, 6), position), (blocks,), jnp.float32, least / len(cuts), top_value / len(cuts))
        factor_of = factor_of * jnp.repeat(jnp.exp(steps), dims[position] // blocks).reshape((-1,) + (1,) * (len(dims) - 1 - position))
    return factor_of


def bell_draw(rng, extent, scale, limit, cuts=(), kind=jnp.bfloat16):
    result = jax.random.normal(rng, extent, jnp.float32) * scale
    if len(cuts) > 0:
        result = levels(rng, extent, cuts, -0.22, 0.18) * result
    return jnp.clip(result, min=-limit, max=limit).astype(kind)


def setup_inputs(seed: int = 0) -> dict:
    key_list = jax.random.split(jax.random.key(seed), 9)
    return {
        "latent": bell_draw(key_list[0], (MEMBERS, BATCH, POINTS, H), 1.0, 6.0, ((0, 16), (1, 2), (2, 16))),
        "target": bell_draw(key_list[1], (BATCH, C, POINTS), 1.0, 6.0, ((0, 2), (2, 16))),
        "weight": bell_draw(key_list[2], (C, H), H ** -0.5, 0.1875),
        "bias": bell_draw(key_list[3], (C,), 0.5, 3.0, (), jnp.float32),
        "gain": jnp.clip(1.0 + 0.18 * jax.random.normal(key_list[4], (H,), jnp.float32), 0.1, 1.9),
        "channel_weight": jnp.clip(jnp.exp(jax.random.uniform(key_list[5], (C,), jnp.float32, math.log(0.25), math.log(4.0))), 0.25, 4.0),
        "band_offsets": draw_band_offsets(jax.random.fold_in(key_list[8], 71), 0),
        "row_points": draw_row_points(jax.random.fold_in(key_list[8], 71), 0),
    }


smooth_sq = 0.01

def smooth_abs(value):
    return jnp.sqrt(value * value + smooth_sq)

def smooth_sign(value):
    return value / jnp.sqrt(value * value + smooth_sq)

def normalize(samples, gain):
    values = samples.astype(jnp.float32)
    middle = lax.optimization_barrier(jnp.mean(values, axis=-1, keepdims=True))
    centered = values - middle
    variance = lax.optimization_barrier(jnp.mean(centered * centered, axis=-1, keepdims=True))
    inverse = lax.rsqrt(variance + 1e-05)
    unit_rows = centered * inverse
    scaled = (unit_rows * gain).astype(jnp.bfloat16)
    return (unit_rows, inverse, scaled)

def reference(latent, target, weight, bias, gain, channel_weight, band_offsets, row_points):
    row_ids = jnp.arange(LAT_ROWS, dtype=jnp.int32)
    in_band = (row_ids[None, :] >= band_offsets[:-1, None]) & (row_ids[None, :] < band_offsets[1:, None])
    counts = lax.optimization_barrier(jnp.sum(jnp.where(in_band, row_points[None, :], 0), axis=1)).astype(jnp.int32)
    slot_ids = jnp.arange(POINTS, dtype=jnp.int32)
    limits = counts[slot_ids // PTS_DEV]
    live = (slot_ids % PTS_DEV < limits).astype(jnp.float32)
    total_live = jnp.sum(counts).astype(jnp.float32)
    weight_f = weight.astype(jnp.float32)

    def forward(samples):
        unit_rows, inverse, scaled = normalize(samples, gain)
        out = jnp.einsum('bph,ch->bcp', scaled.astype(jnp.float32), weight_f, precision=lax.Precision.HIGHEST)
        return out + bias[None, :, None]
    predicted = lax.map(forward, latent)
    observed = target.astype(jnp.float32)
    grid_weight = channel_weight[None, :, None] * live[None, None, :]
    pair_weight = 1.0 / (MEMBERS - 1)
    score = jnp.float32(0.0)
    slopes = []
    for member in range(MEMBERS):
        error = predicted[member] - observed
        others = (jnp.arange(MEMBERS) != member).astype(jnp.float32)[:, None, None, None]
        spread_gap = predicted[member][None] - predicted
        spread = lax.optimization_barrier(jnp.sum(others * smooth_abs(spread_gap), axis=0))
        pair_slope = lax.optimization_barrier(jnp.sum(others * smooth_sign(spread_gap), axis=0))
        score = score + jnp.sum(grid_weight * (smooth_abs(error) - 0.5 * pair_weight * spread))
        slopes.append(grid_weight * (smooth_sign(error) - pair_weight * pair_slope))
    dpred = jnp.stack(slopes)

    def backward(pair):
        samples, member_grad = pair
        unit_rows, inverse, scaled = normalize(samples, gain)
        grad_low = member_grad.astype(jnp.bfloat16).astype(jnp.float32)
        grad_w = jnp.einsum('bcp,bph->ch', grad_low, scaled.astype(jnp.float32), precision=lax.Precision.HIGHEST)
        grad_b = lax.optimization_barrier(jnp.sum(member_grad, axis=(0, 2)))
        dscaled = jnp.einsum('bcp,ch->bph', grad_low, weight_f, precision=lax.Precision.HIGHEST)
        grad_g = lax.optimization_barrier(jnp.sum(dscaled * unit_rows, axis=(0, 1)))
        dunit = dscaled * gain
        first = lax.optimization_barrier(jnp.mean(dunit, axis=-1, keepdims=True))
        second = lax.optimization_barrier(jnp.mean(dunit * unit_rows, axis=-1, keepdims=True))
        grad_x = (inverse * (dunit - first - unit_rows * second)).astype(jnp.bfloat16)
        return (grad_x, grad_w, grad_b, grad_g)
    grad_latent, grad_ws, grad_bs, grad_gs = lax.map(backward, (latent, dpred))
    loss = score / (C * BATCH * total_live)
    return (grad_latent, lax.optimization_barrier(jnp.sum(grad_ws, axis=0)), lax.optimization_barrier(jnp.sum(grad_bs, axis=0)), lax.optimization_barrier(jnp.sum(grad_gs, axis=0)), loss)
```

```python
import jax
import jax.numpy as jnp
from jax import lax
from jax.experimental import pallas as pl
from jax.experimental.pallas import tpu as pltpu
from jax.sharding import PartitionSpec as P

MESH = pl.DeviceIdType.MESH
F32 = jnp.float32
BF16 = jnp.bfloat16
H, C, PTS = 1024, 100, 1024
MEMBERS, NX, NY, NZ, YLO = 16, 4, 8, 8, 4
HALF, LANES, BLOCKS = 56, 128, 8
SMOOTH = 0.01


def remote(src, dst, send, recv, where):
    return pltpu.make_async_remote_copy(
        src_ref=src, dst_ref=dst, send_sem=send, recv_sem=recv, device_id=where, device_id_type=MESH
    )


def kernel(
    lat, tgt, weight, bias, gain, chan, live,
    out_lat, out_w, out_g, out_x,
    wpad, wgain, bcol, qcol, rows, tpad, bsum,
    scaled, s_mean, s_inv, pred, got, back, grads, dlow,
    full, r_core, sum_core, r_x, sum_x, r_y, sum_y, r_z, final,
    a_send, a_recv, b_send, b_recv, c_sem, x_send, x_recv, y_send, y_recv,
    z_send, z_recv, gy_send, gy_recv, gx_send, gx_recv, gc_sem,
):
    me = lax.axis_index("member")
    sp = lax.axis_index("space")
    dp = lax.axis_index("dp")
    my_x, y_lo = me // YLO, me % YLO
    my_y = dp * YLO + y_lo
    my_z, core = sp // 2, sp % 2
    far = (dp + 1) % 2
    mate = my_z * 2 + (1 - core)
    block, half = me // 2, me % 2

    barrier = pltpu.get_barrier_semaphore()

    @pl.loop(1, MEMBERS)
    def _(i):
        pl.semaphore_signal(barrier, inc=1, device_id={"member": (me + i) % MEMBERS}, device_id_type=MESH)

    @pl.loop(0, YLO)
    def _(i):
        pl.semaphore_signal(
            barrier, inc=1, device_id={"member": my_x * YLO + i, "dp": far}, device_id_type=MESH
        )

    @pl.loop(1, NZ)
    def _(i):
        pl.semaphore_signal(
            barrier, inc=1, device_id={"space": ((my_z + i) % NZ) * 2 + core}, device_id_type=MESH
        )

    pl.semaphore_signal(barrier, inc=1, device_id={"space": mate}, device_id_type=MESH)

    wpad[96:128, :] = jnp.zeros((32, H), BF16)
    wpad[0:C, :] = weight[...]
    rows[...] = jnp.zeros((16, LANES), F32)
    rows[0:1, 0:C] = bias[...]
    rows[8:9, 0:C] = chan[...]
    bcol[...] = jnp.transpose(jnp.broadcast_to(rows[0:1, :], (LANES, LANES)))
    qcol[...] = jnp.transpose(jnp.broadcast_to(rows[8:9, :], (LANES, LANES)))
    pl.semaphore_wait(barrier, (MEMBERS - 1) + YLO + (NZ - 1) + 1)

    @pl.loop(0, BLOCKS)
    def _(i):
        j = (block + 1 + i) % BLOCKS
        pts = pl.ds(pl.multiple_of(j * LANES, LANES), LANES)
        values = lat[pts, :].astype(F32)
        mean = jnp.sum(values, axis=1, keepdims=True) * (1.0 / H)
        centered = values - mean
        var = jnp.sum(centered * centered, axis=1, keepdims=True) * (1.0 / H)
        inv = lax.rsqrt(var + 1e-05)
        low = ((centered * inv) * gain[...]).astype(BF16)
        scaled[pts, :] = low
        s_mean[pts, :] = mean
        s_inv[pts, :] = inv
        out = lax.dot_general(
            wpad[0 : 2 * HALF, :], low, (((1,), (1,)), ((), ())), preferred_element_type=F32
        )
        out = out + bcol[0 : 2 * HALF, :]
        for r in range(2):
            k = 2 * j + r
            pred[k] = out[r * HALF : (r + 1) * HALF]

            @pl.when(k != me)
            def _():
                remote(pred.at[k], got.at[me], a_send.at[k], a_recv.at[me], {"member": k}).start()

    mine = pl.ds(pl.multiple_of(block * LANES, LANES), LANES)
    tpad[96:112, :] = jnp.zeros((16, LANES), F32)
    tpad[0:C, :] = tgt[:, mine].astype(F32)
    bsum[...] = jnp.zeros((LANES, LANES), F32)
    got[me] = pred[me]

    wg = wpad[...].astype(F32) * gain[...]
    wgain[...] = (wg - jnp.sum(wg, axis=1, keepdims=True) * (1.0 / H)).astype(BF16)

    @pl.loop(1, MEMBERS)
    def _(i):
        k = (me + i) % MEMBERS
        remote(pred.at[k], got.at[k], a_send.at[k], a_recv.at[k], {"member": k}).wait()

    live_row = live[0:1, mine]
    pair = 1.0 / (MEMBERS - 1)

    def tile(t, score):
        row = pl.multiple_of(t * 8, 8)
        here = pl.ds(row, 8)
        band = pl.ds(pl.multiple_of(half * HALF + row, 8), 8)
        q = qcol[band, :] * live_row
        obs = tpad[band, :]
        p = [got[m, here, :] for m in range(MEMBERS)]
        slope = [None] * MEMBERS
        spread = jnp.zeros((8, LANES), F32)
        for m in range(MEMBERS):
            for n in range(m + 1, MEMBERS):
                gap = p[m] - p[n]
                square = gap * gap + SMOOTH
                root = lax.rsqrt(square)
                spread = spread + square * root
                sign = gap * root
                slope[m] = sign if slope[m] is None else slope[m] + sign
                slope[n] = -sign if slope[n] is None else slope[n] - sign
        skill = jnp.zeros((8, LANES), F32)
        total = jnp.zeros((8, LANES), F32)
        for m in range(MEMBERS):
            gap = p[m] - obs
            square = gap * gap + SMOOTH
            root = lax.rsqrt(square)
            skill = skill + square * root
            sign = gap * root
            total = total + sign
            back[m, here, :] = q * (sign - pair * slope[m])
        bsum[band, :] = q * total
        return score + q * (skill - pair * spread)

    score = lax.fori_loop(0, HALF // 8, tile, jnp.zeros((8, LANES), F32))
    score = jnp.sum(jnp.sum(score, axis=1, keepdims=True), axis=0, keepdims=True)

    @pl.loop(1, MEMBERS)
    def _(i):
        k = (me + i) % MEMBERS
        remote(back.at[k], grads.at[me], b_send.at[k], b_recv.at[me], {"member": k}).start()

    grads[me] = back[me]
    bias_row = jnp.sum(jnp.transpose(bsum[...]), axis=0, keepdims=True)
    row_id = lax.broadcasted_iota(jnp.int32, (16, LANES), 0)
    for y in range(NY):
        full[1, 3, y] = jnp.zeros((16, LANES), F32)
    full[1, 3, 0] = jnp.where(row_id == 0, bias_row, jnp.where(row_id == 1, score, 0.0))

    @pl.loop(1, MEMBERS)
    def _(i):
        k = (me + i) % MEMBERS
        remote(back.at[k], grads.at[k], b_send.at[k], b_recv.at[k], {"member": k}).wait()

    for j in range(BLOCKS):
        pts = slice(j * LANES, (j + 1) * LANES)
        dlow[0:HALF, pts] = grads[2 * j]
        dlow[HALF : 2 * HALF, pts] = grads[2 * j + 1]

    dl = dlow[...].astype(BF16)
    for y in range(NY):
        gw = jnp.dot(dl, scaled[:, y * LANES : (y + 1) * LANES], preferred_element_type=F32)
        for g in range(7):
            full[g // 4, g % 4, y] = gw[g * 16 : (g + 1) * 16]

    core_copy = remote(full.at[1 - core], r_core, c_sem.at[0], c_sem.at[1], {"space": mate})
    core_copy.start()

    def latent_block(j):
        pts = pl.ds(pl.multiple_of(j * LANES, LANES), LANES)
        d = dlow[:, pts].astype(BF16).astype(F32)
        plain = jnp.concatenate([pred[2 * j], pred[2 * j + 1]], axis=0) - bcol[0 : 2 * HALF, :]
        second = jnp.sum(d * plain, axis=0, keepdims=True) * (1.0 / H)
        second = jnp.transpose(jnp.broadcast_to(second, (LANES, LANES)))[:, 0:1]
        d = jnp.concatenate([d, jnp.zeros((16, LANES), F32)], axis=0)
        dunit = jnp.dot(jnp.transpose(d).astype(BF16), wgain[...], preferred_element_type=F32)
        inv = s_inv[pts, :]
        unit = (lat[pts, :].astype(F32) - s_mean[pts, :]) * inv
        out_lat[pts, :] = (inv * (dunit - unit * second)).astype(BF16)

    pl.loop(0, 1)(latent_block)
    core_copy.wait()

    for x in range(NX):
        sum_core[x] = full[core, x] + r_core[x]

    @pl.loop(1, NX)
    def _(i):
        k = (my_x + i) % NX
        remote(
            sum_core.at[k], r_x.at[my_x], x_send.at[k], x_recv.at[my_x], {"member": k * YLO + y_lo}
        ).start()

    r_x[my_x] = sum_core[my_x]
    pl.loop(1, 4)(latent_block)

    @pl.loop(1, NX)
    def _(i):
        k = (my_x + i) % NX
        remote(
            sum_core.at[k], r_x.at[k], x_send.at[k], x_recv.at[k], {"member": k * YLO + y_lo}
        ).wait()

    sum_x[...] = (r_x[0] + r_x[1]) + (r_x[2] + r_x[3])

    def at_y(k):
        return {"member": my_x * YLO + k % YLO, "dp": k // YLO}

    @pl.loop(1, NY)
    def _(i):
        k = (my_y + i) % NY
        remote(sum_x.at[k], r_y.at[my_y], y_send.at[k], y_recv.at[my_y], at_y(k)).start()

    r_y[my_y] = sum_x[my_y]
    pl.loop(4, 6)(latent_block)

    @pl.loop(1, NY)
    def _(i):
        k = (my_y + i) % NY
        remote(sum_x.at[k], r_y.at[k], y_send.at[k], y_recv.at[k], at_y(k)).wait()

    sum_y[...] = jnp.sum(r_y[...], axis=0)

    @pl.loop(1, NZ)
    def _(i):
        k = (my_z + i) % NZ
        remote(sum_y, r_z.at[my_z], z_send.at[k], z_recv.at[my_z], {"space": k * 2 + core}).start()

    r_z[my_z] = sum_y[...]
    pl.loop(6, 8)(latent_block)

    @pl.loop(1, NZ)
    def _(i):
        k = (my_z + i) % NZ
        remote(sum_y, r_z.at[k], z_send.at[k], z_recv.at[k], {"space": k * 2 + core}).wait()

    final[core, my_x, my_y] = jnp.sum(r_z[...], axis=0)

    @pl.loop(1, NY)
    def _(i):
        k = (my_y + i) % NY
        piece = final.at[core, my_x, my_y]
        remote(piece, piece, gy_send.at[k], gy_recv.at[my_y], at_y(k)).start()

    @pl.loop(1, NY)
    def _(i):
        k = (my_y + i) % NY
        remote(
            final.at[core, my_x, my_y], final.at[core, my_x, k], gy_send.at[k], gy_recv.at[k], at_y(k)
        ).wait()

    @pl.loop(1, NX)
    def _(i):
        k = (my_x + i) % NX
        piece = final.at[core, my_x]
        remote(piece, piece, gx_send.at[k], gx_recv.at[my_x], {"member": k * YLO + y_lo}).start()

    @pl.loop(1, NX)
    def _(i):
        k = (my_x + i) % NX
        remote(
            final.at[core, my_x], final.at[core, k], gx_send.at[k], gx_recv.at[k],
            {"member": k * YLO + y_lo},
        ).wait()

    last = remote(final.at[core], final.at[core], gc_sem.at[0], gc_sem.at[1], {"space": mate})
    last.start()
    last.wait_send()
    remote(final.at[core], final.at[1 - core], gc_sem.at[0], gc_sem.at[1], {"space": mate}).wait_recv()

    for y in range(NY):
        cols = slice(y * LANES, (y + 1) * LANES)
        acc = jnp.zeros((16, LANES), F32)
        for g in range(7):
            piece = final[g // 4, g % 4, y]
            top = min(16, C - g * 16)
            out_w[g * 16 : g * 16 + top, cols] = piece[0:top]
            acc = acc + piece * wpad[g * 16 : (g + 1) * 16, cols].astype(F32)
        out_g[0:1, cols] = jnp.sum(acc, axis=0, keepdims=True) / gain[0:1, cols]
    out_x[...] = final[1, 3, 0]


def shards(latent, target, weight, bias, gain, channel_weight, band_offsets, row_points):
    bands = lax.axis_size("space")
    band = lax.axis_index("space")
    row_ids = jnp.arange(row_points.shape[0], dtype=jnp.int32)
    in_band = (row_ids[None, :] >= band_offsets[:-1, None]) & (
        row_ids[None, :] < band_offsets[1:, None]
    )
    counts = jnp.sum(jnp.where(in_band, row_points[None, :], 0), axis=1)
    live_count = jnp.sum(jnp.where(jnp.arange(bands, dtype=jnp.int32) == band, counts, 0))
    total_live = jnp.sum(counts).astype(F32)
    live = (jnp.arange(PTS, dtype=jnp.int32) < live_count).astype(F32)
    vmem = pl.BlockSpec(memory_space=pltpu.VMEM)

    def buf(*shape, kind=F32):
        return pltpu.VMEM(shape, kind)

    def sems(n):
        return pltpu.SemaphoreType.DMA((n,))

    grad_x, sum_w, sum_g, extra = pl.pallas_call(
        kernel,
        name="crps_head",
        out_shape=(
            jax.ShapeDtypeStruct((PTS, H), BF16),
            jax.ShapeDtypeStruct((C, H), F32),
            jax.ShapeDtypeStruct((1, H), F32),
            jax.ShapeDtypeStruct((16, LANES), F32),
        ),
        in_specs=[vmem] * 7,
        out_specs=(vmem,) * 4,
        scratch_shapes=[
            buf(LANES, H, kind=BF16), buf(LANES, H, kind=BF16),
            buf(LANES, LANES), buf(LANES, LANES), buf(16, LANES), buf(2 * HALF, LANES),
            buf(LANES, LANES),
            buf(PTS, H, kind=BF16), buf(PTS, 1), buf(PTS, 1),
            buf(MEMBERS, HALF, LANES), buf(MEMBERS, HALF, LANES),
            buf(MEMBERS, HALF, LANES), buf(MEMBERS, HALF, LANES),
            buf(2 * HALF, PTS),
            buf(2, NX, NY, 16, LANES), buf(NX, NY, 16, LANES), buf(NX, NY, 16, LANES),
            buf(NX, NY, 16, LANES), buf(NY, 16, LANES), buf(NY, 16, LANES),
            buf(16, LANES), buf(NZ, 16, LANES), buf(2, NX, NY, 16, LANES),
            sems(MEMBERS), sems(MEMBERS), sems(MEMBERS), sems(MEMBERS), sems(2),
            sems(NX), sems(NX), sems(NY), sems(NY), sems(NZ), sems(NZ),
            sems(NY), sems(NY), sems(NX), sems(NX), sems(2),
        ],
        compiler_params=pltpu.CompilerParams(collective_id=0, has_side_effects=True),
    )(
        latent.reshape(PTS, H), target[0], weight, bias[None], gain[None], channel_weight[None],
        live[None],
    )
    batch = lax.axis_size("dp")
    loss = extra[1, 0] / (C * batch * total_live)
    return (grad_x[None, None], sum_w, extra[0, :C], sum_g[0], loss)


def solution(mesh):
    return jax.shard_map(
        shards,
        mesh=mesh,
        in_specs=(
            P("member", "dp", "space", None),
            P("dp", None, "space"),
            P(), P(), P(), P(), P(), P(),
        ),
        out_specs=(P("member", "dp", "space", None), P(), P(), P(), P()),
        check_vma=False,
    )
```

```python
import jax
import jax.numpy as jnp
from jax import lax
from jax.experimental import pallas as pl
from jax.experimental.pallas import tpu as pltpu
from jax.sharding import PartitionSpec as P

MESH = pl.DeviceIdType.MESH
F32 = jnp.float32
BF16 = jnp.bfloat16
H, C, PTS = 1024, 100, 1024
MEMBERS, NX, NY, NZ, YLO = 16, 4, 8, 8, 4
HALF, LANES, BLOCKS, PIECES = 56, 128, 8, 7
SMOOTH = 0.01


def remote(src, dst, send, recv, where):
    return pltpu.make_async_remote_copy(
        src_ref=src, dst_ref=dst, send_sem=send, recv_sem=recv, device_id=where, device_id_type=MESH
    )


def kernel(
    lat_in, tgt, weight, bias, gain, chan, offsets, row_points,
    out_lat, out_w, out_g, out_b, out_loss,
    lat, tbuf,
    wpad, wgain, bcol, qcol, rows, tpad, bsum,
    scaled, s_mean, s_inv, pred, got, back, grads, dlow,
    full, r_core, sum_core, r_x, sum_x, r_y, sum_y, r_z, final,
    l_sem, t_sem, a_send, a_recv, b_send, b_recv, c_send, c_recv, x_send, x_recv, y_send, y_recv,
    z_send, z_recv, gy_send, gx_send, g_recv, gm_send, gm_recv,
):
    me = lax.axis_index("member")
    sp = lax.axis_index("space")
    dp = lax.axis_index("dp")
    my_x, y_lo = me // YLO, me % YLO
    my_y = dp * YLO + y_lo
    my_z, core = sp // 2, sp % 2
    far = (dp + 1) % 2
    mate = my_z * 2 + (1 - core)
    block, half = me // 2, me % 2

    barrier = pltpu.get_barrier_semaphore()

    @pl.loop(1, MEMBERS)
    def _(i):
        pl.semaphore_signal(barrier, inc=1, device_id={"member": (me + i) % MEMBERS}, device_id_type=MESH)

    @pl.loop(0, YLO)
    def _(i):
        pl.semaphore_signal(
            barrier, inc=1, device_id={"member": my_x * YLO + i, "dp": far}, device_id_type=MESH
        )

    @pl.loop(1, NZ)
    def _(i):
        pl.semaphore_signal(
            barrier, inc=1, device_id={"space": ((my_z + i) % NZ) * 2 + core}, device_id_type=MESH
        )

    pl.semaphore_signal(barrier, inc=1, device_id={"space": mate}, device_id_type=MESH)

    def load(i):
        j = (block + 1 + i) % BLOCKS
        pts = pl.ds(pl.multiple_of(j * LANES, LANES), LANES)
        return pltpu.make_async_copy(lat_in.at[pts, :], lat.at[pts, :], l_sem.at[j])

    @pl.loop(0, BLOCKS)
    def _(i):
        load(i).start()

    mine = pl.ds(pl.multiple_of(block * LANES, LANES), LANES)
    load_target = pltpu.make_async_copy(tgt.at[:, mine], tbuf, t_sem)
    load_target.start()

    wpad[96:128, :] = jnp.zeros((32, H), BF16)
    wpad[0:C, :] = weight[...]
    rows[...] = jnp.zeros((16, LANES), F32)
    rows[0:1, 0:C] = bias[...]
    rows[8:9, 0:C] = chan[...]
    bcol[...] = jnp.transpose(jnp.broadcast_to(rows[0:1, :], (LANES, LANES)))
    qcol[...] = jnp.transpose(jnp.broadcast_to(rows[8:9, :], (LANES, LANES)))
    pl.semaphore_wait(barrier, (MEMBERS - 1) + YLO + (NZ - 1) + 1)

    @pl.loop(0, BLOCKS)
    def _(i):
        j = (block + 1 + i) % BLOCKS
        pts = pl.ds(pl.multiple_of(j * LANES, LANES), LANES)
        load(i).wait()
        values = lat[pts, :].astype(F32)
        mean = jnp.sum(values, axis=1, keepdims=True) * (1.0 / H)
        centered = values - mean
        var = jnp.sum(centered * centered, axis=1, keepdims=True) * (1.0 / H)
        inv = lax.rsqrt(var + 1e-05)
        low = ((centered * inv) * gain[...]).astype(BF16)
        scaled[pts, :] = low
        s_mean[pts, :] = mean
        s_inv[pts, :] = inv
        out = lax.dot_general(
            wpad[0 : 2 * HALF, :], low, (((1,), (1,)), ((), ())), preferred_element_type=F32
        )
        out = out + bcol[0 : 2 * HALF, :]
        for r in range(2):
            k = 2 * j + r
            pred[k] = out[r * HALF : (r + 1) * HALF]

            @pl.when(k != me)
            def _():
                remote(pred.at[k], got.at[me], a_send.at[k], a_recv.at[me], {"member": k}).start()

    load_target.wait()
    tpad[96:112, :] = jnp.zeros((16, LANES), F32)
    tpad[0:C, :] = tbuf[...].astype(F32)
    bsum[...] = jnp.zeros((LANES, LANES), F32)
    got[me] = pred[me]

    row_ids = lax.broadcasted_iota(jnp.int32, (1, LANES), 1)
    counts = row_points[...].astype(F32)
    in_band = (row_ids >= offsets[sp]) & (row_ids < offsets[sp + 1])
    live_count = jnp.sum(jnp.where(in_band, counts, 0.0), axis=1, keepdims=True)
    total_live = jnp.sum(jnp.where(row_ids < offsets[16], counts, 0.0), axis=1, keepdims=True)
    live_row = ((row_ids + block * LANES).astype(F32) < live_count).astype(F32)

    wg = wpad[...].astype(F32) * gain[...]
    wgain[...] = (wg - jnp.sum(wg, axis=1, keepdims=True) * (1.0 / H)).astype(BF16)

    @pl.loop(1, MEMBERS)
    def _(i):
        k = (me + i) % MEMBERS
        remote(pred.at[k], got.at[k], a_send.at[k], a_recv.at[k], {"member": k}).wait()

    pair = 1.0 / (MEMBERS - 1)

    def tile(t, score):
        row = pl.multiple_of(t * 8, 8)
        here = pl.ds(row, 8)
        band = pl.ds(pl.multiple_of(half * HALF + row, 8), 8)
        q = qcol[band, :] * live_row
        obs = tpad[band, :]
        p = [got[m, here, :] for m in range(MEMBERS)]
        slope = [None] * MEMBERS
        spread = jnp.zeros((8, LANES), F32)
        for m in range(MEMBERS):
            for n in range(m + 1, MEMBERS):
                gap = p[m] - p[n]
                square = gap * gap + SMOOTH
                root = lax.rsqrt(square)
                spread = spread + square * root
                sign = gap * root
                slope[m] = sign if slope[m] is None else slope[m] + sign
                slope[n] = -sign if slope[n] is None else slope[n] - sign
        skill = jnp.zeros((8, LANES), F32)
        total = jnp.zeros((8, LANES), F32)
        for m in range(MEMBERS):
            gap = p[m] - obs
            square = gap * gap + SMOOTH
            root = lax.rsqrt(square)
            skill = skill + square * root
            sign = gap * root
            total = total + sign
            back[m, here, :] = q * (sign - pair * slope[m])
        bsum[band, :] = q * total
        return score + q * (skill - pair * spread)

    score = lax.fori_loop(0, HALF // 8, tile, jnp.zeros((8, LANES), F32))
    score = jnp.sum(jnp.sum(score, axis=1, keepdims=True), axis=0, keepdims=True)

    @pl.loop(1, MEMBERS)
    def _(i):
        k = (me + i) % MEMBERS
        remote(back.at[k], grads.at[me], b_send.at[k], b_recv.at[me], {"member": k}).start()

    grads[me] = back[me]
    bias_row = jnp.sum(jnp.transpose(bsum[...]), axis=0, keepdims=True)
    row_id = lax.broadcasted_iota(jnp.int32, (16, LANES), 0)
    extra = jnp.where(row_id == 4, bias_row, jnp.where(row_id == 5, score, 0.0))

    @pl.loop(1, MEMBERS)
    def _(i):
        k = (me + i) % MEMBERS
        remote(back.at[k], grads.at[k], b_send.at[k], b_recv.at[k], {"member": k}).wait()

    for j in range(BLOCKS):
        pts = slice(j * LANES, (j + 1) * LANES)
        dlow[0:HALF, pts] = grads[2 * j]
        dlow[HALF : 2 * HALF, pts] = grads[2 * j + 1]

    dl = dlow[...].astype(BF16)
    for tile_id in range(8):
        gw = jnp.dot(
            dl, scaled[:, tile_id * LANES : (tile_id + 1) * LANES], preferred_element_type=F32
        )
        for g in range(PIECES):
            piece = gw[g * 16 : (g + 1) * 16]
            if tile_id == 0 and g == 6:
                piece = piece + extra
            full[tile_id // 4, tile_id % 4, g] = piece

    def to_mate(x):
        return remote(
            full.at[1 - core, x], r_core.at[x], c_send.at[x], c_recv.at[x], {"space": mate}
        )

    def to_x(k, slot):
        return remote(
            sum_core.at[k], r_x.at[slot], x_send.at[k], x_recv.at[slot], {"member": k * YLO + y_lo}
        )

    @pl.loop(1, NX + 1)
    def _(i):
        to_mate((my_x + i) % NX).start()

    def latent_block(j):
        pts = pl.ds(pl.multiple_of(j * LANES, LANES), LANES)
        d = dlow[:, pts].astype(BF16).astype(F32)
        plain = jnp.concatenate([pred[2 * j], pred[2 * j + 1]], axis=0) - bcol[0 : 2 * HALF, :]
        second = jnp.sum(d * plain, axis=0, keepdims=True) * (1.0 / H)
        second = jnp.transpose(jnp.broadcast_to(second, (LANES, LANES)))[:, 0:1]
        d = jnp.concatenate([d, jnp.zeros((16, LANES), F32)], axis=0)
        dunit = jnp.dot(jnp.transpose(d).astype(BF16), wgain[...], preferred_element_type=F32)
        inv = s_inv[pts, :]
        unit = (lat[pts, :].astype(F32) - s_mean[pts, :]) * inv
        out_lat[pts, :] = (inv * (dunit - unit * second)).astype(BF16)

    pl.loop(0, 1)(latent_block)

    @pl.loop(1, NX)
    def _(i):
        k = (my_x + i) % NX
        to_mate(k).wait()
        sum_core[k] = full[core, k] + r_core[k]
        to_x(k, my_x).start()

    to_mate(my_x).wait()
    r_x[my_x] = full[core, my_x] + r_core[my_x]
    pl.loop(1, 4)(latent_block)

    @pl.loop(1, NX)
    def _(i):
        k = (my_x + i) % NX
        to_x(k, k).wait()

    sum_x[...] = (r_x[0] + r_x[1]) + (r_x[2] + r_x[3])

    def at_y(k):
        return {"member": my_x * YLO + k % YLO, "dp": k // YLO}

    owner = my_y < PIECES

    @pl.loop(1, NY)
    def _(i):
        k = (my_y + i) % NY

        @pl.when(k < PIECES)
        def _():
            remote(sum_x.at[k], r_y.at[my_y], y_send.at[k], y_recv.at[my_y], at_y(k)).start()

    pl.loop(4, 6)(latent_block)

    @pl.loop(1, NY)
    def _(i):
        k = (my_y + i) % NY

        @pl.when(k < PIECES)
        def _():
            remote(sum_x.at[k], r_y.at[my_y], y_send.at[k], y_recv.at[my_y], at_y(k)).wait_send()

        @pl.when(owner)
        def _():
            remote(sum_x.at[0], r_y.at[k], y_send.at[k], y_recv.at[k], at_y(k)).wait_recv()

    @pl.when(owner)
    def _():
        r_y[my_y] = sum_x[my_y]
        sum_y[...] = jnp.sum(r_y[...], axis=0)

        @pl.loop(1, NZ)
        def _(i):
            k = (my_z + i) % NZ
            remote(sum_y, r_z.at[my_z], z_send.at[k], z_recv.at[my_z], {"space": k * 2 + core}).start()

        r_z[my_z] = sum_y[...]

    pl.loop(6, 8)(latent_block)

    def spread_y(k):
        piece = final.at[core, my_x, my_y]
        return remote(piece, piece, gy_send.at[k], g_recv.at[my_x, my_y], at_y(k))

    def spread_x(k, x):
        piece = final.at[core, my_x, k]
        return remote(
            piece, piece, gx_send.at[x, k], g_recv.at[my_x, k], {"member": x * YLO + y_lo}
        )

    def arrived(x, k):
        piece = final.at[core, x, k]
        return remote(piece, piece, gy_send.at[0], g_recv.at[x, k], {"space": mate})

    def spread_mate(x, k):
        piece = final.at[core, x, k]
        return remote(piece, piece, gm_send.at[x, k], gm_recv.at[x, k], {"space": mate})

    def mate_arrived(x, k):
        piece = final.at[1 - core, x, k]
        return remote(piece, piece, gm_send.at[x, k], gm_recv.at[x, k], {"space": mate})

    @pl.when(owner)
    def _():
        @pl.loop(1, NZ)
        def _(i):
            k = (my_z + i) % NZ
            remote(sum_y, r_z.at[k], z_send.at[k], z_recv.at[k], {"space": k * 2 + core}).wait()

        final[core, my_x, my_y] = jnp.sum(r_z[...], axis=0)

        @pl.loop(1, NY)
        def _(i):
            spread_y((my_y + i) % NY).start()

    @pl.loop(0, NY)
    def _(i):
        k = (my_y + i) % NY

        @pl.when(k < PIECES)
        def _():
            @pl.when(i > 0)
            def _():
                arrived(my_x, k).wait_recv()

            @pl.loop(1, NX)
            def _(d):
                spread_x(k, (my_x + d) % NX).start()

            spread_mate(my_x, k).start()

    @pl.loop(0, NY)
    def _(i):
        k = (my_y + i) % NY

        @pl.when(k < PIECES)
        def _():
            @pl.loop(1, NX)
            def _(d):
                x = (my_x + d) % NX
                arrived(x, k).wait_recv()
                spread_mate(x, k).start()

    @pl.when(owner)
    def _():
        @pl.loop(1, NY)
        def _(i):
            spread_y((my_y + i) % NY).wait_send()

    @pl.loop(0, PIECES)
    def _(k):
        @pl.loop(1, NX)
        def _(d):
            spread_x(k, (my_x + d) % NX).wait_send()

        @pl.loop(0, NX)
        def _(x):
            spread_mate(x, k).wait_send()
            mate_arrived(x, k).wait_recv()

    for tile_id in range(8):
        cols = slice(tile_id * LANES, (tile_id + 1) * LANES)
        acc = jnp.zeros((16, LANES), F32)
        for g in range(PIECES):
            piece = final[tile_id // 4, tile_id % 4, g]
            top = min(16, C - g * 16)
            out_w[g * 16 : g * 16 + top, cols] = piece[0:top]
            acc = acc + piece * wpad[g * 16 : (g + 1) * 16, cols].astype(F32)
        out_g[0:1, cols] = jnp.sum(acc, axis=0, keepdims=True) / gain[0:1, cols]
    out_b[...] = final[0, 0, 6, 4:5, 0:C]
    out_loss[...] = final[0, 0, 6, 5:6, 0:1] / (C * 2.0 * total_live)


def shards(latent, target, weight, bias, gain, channel_weight, band_offsets, row_points):
    vmem = pl.BlockSpec(memory_space=pltpu.VMEM)

    def buf(*shape, kind=F32):
        return pltpu.VMEM(shape, kind)

    def sems(*shape):
        return pltpu.SemaphoreType.DMA(shape)

    hbm = pl.BlockSpec(memory_space=pl.ANY)
    smem = pl.BlockSpec(memory_space=pltpu.SMEM)
    grad_x, sum_w, sum_g, sum_b, loss = pl.pallas_call(
        kernel,
        name="crps_head",
        out_shape=(pltpu.VMEM((PTS, H), BF16), pltpu.VMEM((C, H), F32), pltpu.VMEM((1, H), F32), pltpu.VMEM((1, C), F32), pltpu.VMEM((1, 1), F32)),
        in_specs=[hbm, hbm, vmem, vmem, vmem, vmem, smem, vmem],
        out_specs=(vmem,) * 5,
        scratch_shapes=[
            buf(PTS, H, kind=BF16), buf(C, LANES, kind=BF16),
            buf(LANES, H, kind=BF16), buf(LANES, H, kind=BF16),
            buf(LANES, LANES), buf(LANES, LANES), buf(16, LANES), buf(2 * HALF, LANES),
            buf(LANES, LANES),
            buf(PTS, H, kind=BF16), buf(PTS, 1), buf(PTS, 1),
            buf(MEMBERS, HALF, LANES), buf(MEMBERS, HALF, LANES),
            buf(MEMBERS, HALF, LANES), buf(MEMBERS, HALF, LANES),
            buf(2 * HALF, PTS),
            buf(2, NX, PIECES, 16, LANES), buf(NX, PIECES, 16, LANES),
            buf(NX, PIECES, 16, LANES), buf(NX, PIECES, 16, LANES), buf(PIECES, 16, LANES),
            buf(NY, 16, LANES), buf(16, LANES), buf(NZ, 16, LANES), buf(2, NX, PIECES, 16, LANES),
            sems(BLOCKS), pltpu.SemaphoreType.DMA,
            sems(MEMBERS), sems(MEMBERS), sems(MEMBERS), sems(MEMBERS), sems(NX), sems(NX),
            sems(NX), sems(NX), sems(NY), sems(NY), sems(NZ), sems(NZ),
            sems(NY), sems(NX, PIECES), sems(NX, PIECES), sems(NX, PIECES), sems(NX, PIECES),
        ],
        compiler_params=pltpu.CompilerParams(collective_id=0, has_side_effects=True),
    )(
        latent.reshape(PTS, H), target[0], weight, bias[None], gain[None], channel_weight[None],
        band_offsets, row_points[None],
    )
    return (grad_x[None, None], sum_w, sum_b[0], sum_g[0], loss[0, 0])


def solution(mesh):
    return jax.shard_map(
        shards,
        mesh=mesh,
        in_specs=(
            P("member", "dp", "space", None),
            P("dp", None, "space"),
            P(), P(), P(), P(), P(), P(),
        ),
        out_specs=(P("member", "dp", "space", None), P(), P(), P(), P()),
        check_vma=False,
    )
```

```python
import jax
import jax.numpy as jnp
from jax import lax
from jax.experimental import pallas as pl
from jax.experimental.pallas import tpu as pltpu
from jax.sharding import PartitionSpec as P

MESH = pl.DeviceIdType.MESH
F32 = jnp.float32
BF16 = jnp.bfloat16
H, C, PTS = 1024, 100, 1024
MEMBERS, NX, NY, NZ, YLO = 16, 4, 8, 8, 4
HALF, REST, LANES, BLOCKS, PIECES = 56, 48, 128, 8, 7
SMOOTH = 0.01


def remote(src, dst, send, recv, where):
    return pltpu.make_async_remote_copy(
        src_ref=src, dst_ref=dst, send_sem=send, recv_sem=recv, device_id=where, device_id_type=MESH
    )


def kernel(
    lat_in, tgt, weight, bias, gain, chan, offsets, row_points,
    out_lat, out_w, out_g, out_b, out_loss,
    lat, tbuf,
    wpad, wgain, bcol, qcol, rows, tpad, bsum,
    scaled, s_mean, s_inv, pred, got, back, grads, dlow,
    full, r_core, sum_core, r_x, sum_x, r_y, sum_y, r_z, final,
    l_sem, t_sem, a_send, a_recv, b_send, b_recv, c_send, c_recv, x_send, x_recv, y_send, y_recv,
    z_send, z_recv, gy_send, gx_send, gr_send, g_recv, gm_send, gm_recv,
):
    me = lax.axis_index("member")
    sp = lax.axis_index("space")
    dp = lax.axis_index("dp")
    my_x, y_lo = me // YLO, me % YLO
    my_y = dp * YLO + y_lo
    my_z, core = sp // 2, sp % 2
    far = (dp + 1) % 2
    mate = my_z * 2 + (1 - core)
    block, half = me // 2, me % 2

    barrier = pltpu.get_barrier_semaphore()

    @pl.loop(1, MEMBERS)
    def _(i):
        pl.semaphore_signal(barrier, inc=1, device_id={"member": (me + i) % MEMBERS}, device_id_type=MESH)

    @pl.loop(0, YLO)
    def _(i):
        pl.semaphore_signal(
            barrier, inc=1, device_id={"member": my_x * YLO + i, "dp": far}, device_id_type=MESH
        )

    @pl.loop(1, NZ)
    def _(i):
        pl.semaphore_signal(
            barrier, inc=1, device_id={"space": ((my_z + i) % NZ) * 2 + core}, device_id_type=MESH
        )

    pl.semaphore_signal(barrier, inc=1, device_id={"space": mate}, device_id_type=MESH)

    side = y_lo // 2

    def block_at(i):
        return ((my_x + i % 4 + i // 4) % NX) * 2 + (side + 1 + i // 4) % 2

    def member_at(i):
        q = i // 4
        x = (my_x + i % 4 + q // 3) % NX
        return x * YLO + ((side + 1 + q // 2) % 2) * 2 + (y_lo + q + q // 2) % 2

    def part(ref, k, h):
        return ref.at[k] if h == 0 else ref.at[k, 0:REST]

    def load(i):
        j = block_at(i)
        pts = pl.ds(pl.multiple_of(j * LANES, LANES), LANES)
        return pltpu.make_async_copy(lat_in.at[pts, :], lat.at[pts, :], l_sem.at[j])

    @pl.loop(0, BLOCKS)
    def _(i):
        load(i).start()

    mine = pl.ds(pl.multiple_of(block * LANES, LANES), LANES)
    load_target = pltpu.make_async_copy(tgt.at[:, mine], tbuf, t_sem)
    load_target.start()

    wpad[96:128, :] = jnp.zeros((32, H), BF16)
    wpad[0:C, :] = weight[...]
    rows[...] = jnp.zeros((16, LANES), F32)
    rows[0:1, 0:C] = bias[...]
    rows[8:9, 0:C] = chan[...]
    bcol[...] = jnp.transpose(jnp.broadcast_to(rows[0:1, :], (LANES, LANES)))
    qcol[...] = jnp.transpose(jnp.broadcast_to(rows[8:9, :], (LANES, LANES)))
    pl.semaphore_wait(barrier, (MEMBERS - 1) + YLO + (NZ - 1) + 1)

    @pl.loop(0, BLOCKS)
    def _(i):
        j = block_at(i)
        pts = pl.ds(pl.multiple_of(j * LANES, LANES), LANES)
        load(i).wait()
        values = lat[pts, :].astype(F32)
        mean = jnp.sum(values, axis=1, keepdims=True) * (1.0 / H)
        centered = values - mean
        var = jnp.sum(centered * centered, axis=1, keepdims=True) * (1.0 / H)
        inv = lax.rsqrt(var + 1e-05)
        low = ((centered * inv) * gain[...]).astype(BF16)
        scaled[pts, :] = low
        s_mean[pts, :] = mean
        s_inv[pts, :] = inv
        out = lax.dot_general(
            wpad[0 : 2 * HALF, :], low, (((1,), (1,)), ((), ())), preferred_element_type=F32
        )
        out = out + bcol[0 : 2 * HALF, :]
        for r in range(2):
            k = 2 * j + r
            pred[k] = out[r * HALF : (r + 1) * HALF]

            @pl.when(k != me)
            def _():
                remote(part(pred, k, r), part(got, me, r), a_send.at[k], a_recv.at[me], {"member": k}).start()

    load_target.wait()
    tpad[96:112, :] = jnp.zeros((16, LANES), F32)
    tpad[0:C, :] = tbuf[...].astype(F32)
    bsum[...] = jnp.zeros((LANES, LANES), F32)
    got[me] = pred[me]

    row_ids = lax.broadcasted_iota(jnp.int32, (1, LANES), 1)
    counts = row_points[...].astype(F32)
    in_band = (row_ids >= offsets[sp]) & (row_ids < offsets[sp + 1])
    live_count = jnp.sum(jnp.where(in_band, counts, 0.0), axis=1, keepdims=True)
    total_live = jnp.sum(jnp.where(row_ids < offsets[16], counts, 0.0), axis=1, keepdims=True)
    live_row = ((row_ids + block * LANES).astype(F32) < live_count).astype(F32)

    wg = wpad[...].astype(F32) * gain[...]
    wgain[...] = (wg - jnp.sum(wg, axis=1, keepdims=True) * (1.0 / H)).astype(BF16)

    for h in range(2):

        @pl.when(half == h)
        def _():
            @pl.loop(0, MEMBERS - 1)
            def _(i):
                k = member_at(i)
                remote(
                    part(pred, k, h), part(got, k, h), a_send.at[k], a_recv.at[k], {"member": k}
                ).wait_recv()

        @pl.loop(0, BLOCKS)
        def _(i):
            k = 2 * i + h

            @pl.when(k != me)
            def _():
                remote(
                    part(pred, k, h), part(got, k, h), a_send.at[k], a_recv.at[k], {"member": k}
                ).wait_send()

    pair = 1.0 / (MEMBERS - 1)

    def tile(t, score):
        row = pl.multiple_of(t * 8, 8)
        here = pl.ds(row, 8)
        band = pl.ds(pl.multiple_of(half * HALF + row, 8), 8)
        q = qcol[band, :] * live_row
        obs = tpad[band, :]
        p = [got[m, here, :] for m in range(MEMBERS)]
        slope = [None] * MEMBERS
        spread = jnp.zeros((8, LANES), F32)
        for m in range(MEMBERS):
            for n in range(m + 1, MEMBERS):
                gap = p[m] - p[n]
                square = gap * gap + SMOOTH
                root = lax.rsqrt(square)
                spread = spread + square * root
                sign = gap * root
                slope[m] = sign if slope[m] is None else slope[m] + sign
                slope[n] = -sign if slope[n] is None else slope[n] - sign
        skill = jnp.zeros((8, LANES), F32)
        total = jnp.zeros((8, LANES), F32)
        for m in range(MEMBERS):
            gap = p[m] - obs
            square = gap * gap + SMOOTH
            root = lax.rsqrt(square)
            skill = skill + square * root
            sign = gap * root
            total = total + sign
            back[m, here, :] = q * (sign - pair * slope[m])
        bsum[band, :] = q * total
        return score + q * (skill - pair * spread)

    score = lax.fori_loop(0, HALF // 8 - half, tile, jnp.zeros((8, LANES), F32))
    score = jnp.sum(jnp.sum(score, axis=1, keepdims=True), axis=0, keepdims=True)

    for h in range(2):

        @pl.when(half == h)
        def _():
            @pl.loop(0, MEMBERS - 1)
            def _(i):
                k = member_at(i)
                remote(
                    part(back, k, h), part(grads, me, h), b_send.at[k], b_recv.at[me], {"member": k}
                ).start()

    grads[me] = back[me]
    bias_row = jnp.sum(jnp.transpose(bsum[...]), axis=0, keepdims=True)
    row_id = lax.broadcasted_iota(jnp.int32, (16, LANES), 0)
    extra = jnp.where(row_id == 4, bias_row, jnp.where(row_id == 5, score, 0.0))

    for h in range(2):

        @pl.loop(0, BLOCKS)
        def _(i):
            k = 2 * i + h

            @pl.when(k != me)
            def _():
                remote(
                    part(back, k, h), part(grads, k, h), b_send.at[k], b_recv.at[k], {"member": k}
                ).wait_recv()

        @pl.when(half == h)
        def _():
            @pl.loop(0, MEMBERS - 1)
            def _(i):
                k = member_at(i)
                remote(
                    part(back, k, h), part(grads, k, h), b_send.at[k], b_recv.at[k], {"member": k}
                ).wait_send()

    dlow[HALF + REST : 2 * HALF, :] = jnp.zeros((HALF - REST, PTS), F32)
    for j in range(BLOCKS):
        pts = slice(j * LANES, (j + 1) * LANES)
        dlow[0:HALF, pts] = grads[2 * j]
        dlow[HALF : HALF + REST, pts] = grads[2 * j + 1, 0:REST]

    dl = dlow[...].astype(BF16)
    for tile_id in range(8):
        gw = jnp.dot(
            dl, scaled[:, tile_id * LANES : (tile_id + 1) * LANES], preferred_element_type=F32
        )
        for g in range(PIECES):
            piece = gw[g * 16 : (g + 1) * 16]
            if tile_id == 0 and g == 6:
                piece = piece + extra
            full[tile_id // 4, tile_id % 4, g] = piece

    def to_mate(x):
        return remote(
            full.at[1 - core, x], r_core.at[x], c_send.at[x], c_recv.at[x], {"space": mate}
        )

    def to_x(k, slot):
        return remote(
            sum_core.at[k], r_x.at[slot], x_send.at[k], x_recv.at[slot], {"member": k * YLO + y_lo}
        )

    @pl.loop(1, NX + 1)
    def _(i):
        to_mate((my_x + i) % NX).start()

    def latent_block(j):
        pts = pl.ds(pl.multiple_of(j * LANES, LANES), LANES)
        d = dlow[:, pts].astype(BF16).astype(F32)
        plain = jnp.concatenate([pred[2 * j], pred[2 * j + 1]], axis=0) - bcol[0 : 2 * HALF, :]
        second = jnp.sum(d * plain, axis=0, keepdims=True) * (1.0 / H)
        second = jnp.transpose(jnp.broadcast_to(second, (LANES, LANES)))[:, 0:1]
        d = jnp.concatenate([d, jnp.zeros((16, LANES), F32)], axis=0)
        dunit = jnp.dot(jnp.transpose(d).astype(BF16), wgain[...], preferred_element_type=F32)
        inv = s_inv[pts, :]
        unit = (lat[pts, :].astype(F32) - s_mean[pts, :]) * inv
        out_lat[pts, :] = (inv * (dunit - unit * second)).astype(BF16)

    pl.loop(0, 1)(latent_block)

    @pl.loop(1, NX)
    def _(i):
        k = (my_x + i) % NX
        to_mate(k).wait()
        sum_core[k] = full[core, k] + r_core[k]
        to_x(k, my_x).start()

    to_mate(my_x).wait()
    r_x[my_x] = full[core, my_x] + r_core[my_x]
    pl.loop(1, 4)(latent_block)

    @pl.loop(1, NX)
    def _(i):
        k = (my_x + i) % NX
        to_x(k, k).wait()

    sum_x[...] = (r_x[0] + r_x[1]) + (r_x[2] + r_x[3])

    def at_y(k):
        return {"member": my_x * YLO + k % YLO, "dp": k // YLO}

    owner = my_y < PIECES

    @pl.loop(1, NY)
    def _(i):
        k = (my_y + i) % NY

        @pl.when(k < PIECES)
        def _():
            remote(sum_x.at[k], r_y.at[my_y], y_send.at[k], y_recv.at[my_y], at_y(k)).start()

    pl.loop(4, 6)(latent_block)

    @pl.loop(1, NY)
    def _(i):
        k = (my_y + i) % NY

        @pl.when(k < PIECES)
        def _():
            remote(sum_x.at[k], r_y.at[my_y], y_send.at[k], y_recv.at[my_y], at_y(k)).wait_send()

        @pl.when(owner)
        def _():
            remote(sum_x.at[0], r_y.at[k], y_send.at[k], y_recv.at[k], at_y(k)).wait_recv()

    @pl.when(owner)
    def _():
        r_y[my_y] = sum_x[my_y]
        sum_y[...] = jnp.sum(r_y[...], axis=0)

        @pl.loop(1, NZ)
        def _(i):
            k = (my_z + i) % NZ
            remote(sum_y, r_z.at[my_z], z_send.at[k], z_recv.at[my_z], {"space": k * 2 + core}).start()

        r_z[my_z] = sum_y[...]

    pl.loop(6, 8)(latent_block)

    def spread_y(k):
        piece = final.at[core, my_x, my_y]
        return remote(piece, piece, gy_send.at[k], g_recv.at[my_x, my_y], at_y(k))

    def spread_x(k, x):
        piece = final.at[core, my_x, k]
        return remote(
            piece, piece, gx_send.at[x, k], g_recv.at[my_x, k], {"member": x * YLO + y_lo}
        )

    def relay_from(k):
        return (my_x + 3 + 2 * (k % 2)) % NX

    def relay(k):
        x = (my_x + 1 + 2 * (k % 2)) % NX
        piece = final.at[core, relay_from(k), k]
        return remote(
            piece, piece, gr_send.at[k], g_recv.at[relay_from(k), k], {"member": x * YLO + y_lo}
        )

    def arrived(x, k):
        piece = final.at[core, x, k]
        return remote(piece, piece, gy_send.at[0], g_recv.at[x, k], {"space": mate})

    def spread_mate(x, k):
        piece = final.at[core, x, k]
        return remote(piece, piece, gm_send.at[x, k], gm_recv.at[x, k], {"space": mate})

    def mate_arrived(x, k):
        piece = final.at[1 - core, x, k]
        return remote(piece, piece, gm_send.at[x, k], gm_recv.at[x, k], {"space": mate})

    @pl.when(owner)
    def _():
        @pl.loop(1, NZ)
        def _(i):
            k = (my_z + i) % NZ
            remote(sum_y, r_z.at[k], z_send.at[k], z_recv.at[k], {"space": k * 2 + core}).wait()

        final[core, my_x, my_y] = jnp.sum(r_z[...], axis=0)

        @pl.loop(1, NY)
        def _(i):
            spread_y((my_y + i) % NY).start()

    @pl.loop(0, NY)
    def _(i):
        k = (my_y + i) % NY

        @pl.when(k < PIECES)
        def _():
            @pl.when(i > 0)
            def _():
                arrived(my_x, k).wait_recv()

            @pl.loop(1, NX, step=2)
            def _(d):
                spread_x(k, (my_x + d) % NX).start()

            spread_mate(my_x, k).start()

    @pl.loop(0, NY)
    def _(i):
        k = (my_y + i) % NY

        @pl.when(k < PIECES)
        def _():
            @pl.loop(1, NX, step=2)
            def _(d):
                x = (my_x + d) % NX
                arrived(x, k).wait_recv()

                @pl.when(x == relay_from(k))
                def _():
                    relay(k).start()

                spread_mate(x, k).start()

    @pl.loop(0, NY)
    def _(i):
        k = (my_y + i) % NY

        @pl.when(k < PIECES)
        def _():
            x = (my_x + 2) % NX
            arrived(x, k).wait_recv()
            spread_mate(x, k).start()

    @pl.when(owner)
    def _():
        @pl.loop(1, NY)
        def _(i):
            spread_y((my_y + i) % NY).wait_send()

    @pl.loop(0, PIECES)
    def _(k):
        @pl.loop(1, NX, step=2)
        def _(d):
            spread_x(k, (my_x + d) % NX).wait_send()

        relay(k).wait_send()

        @pl.loop(0, NX)
        def _(x):
            spread_mate(x, k).wait_send()
            mate_arrived(x, k).wait_recv()

    for tile_id in range(8):
        cols = slice(tile_id * LANES, (tile_id + 1) * LANES)
        acc = jnp.zeros((16, LANES), F32)
        for g in range(PIECES):
            piece = final[tile_id // 4, tile_id % 4, g]
            top = min(16, C - g * 16)
            out_w[g * 16 : g * 16 + top, cols] = piece[0:top]
            acc = acc + piece * wpad[g * 16 : (g + 1) * 16, cols].astype(F32)
        out_g[0:1, cols] = jnp.sum(acc, axis=0, keepdims=True) / gain[0:1, cols]
    out_b[...] = final[0, 0, 6, 4:5, 0:C]
    out_loss[...] = final[0, 0, 6, 5:6, 0:1] / (C * 2.0 * total_live)


def shards(latent, target, weight, bias, gain, channel_weight, band_offsets, row_points):
    vmem = pl.BlockSpec(memory_space=pltpu.VMEM)

    def buf(*shape, kind=F32):
        return pltpu.VMEM(shape, kind)

    def sems(*shape):
        return pltpu.SemaphoreType.DMA(shape)

    hbm = pl.BlockSpec(memory_space=pl.ANY)
    smem = pl.BlockSpec(memory_space=pltpu.SMEM)
    grad_x, sum_w, sum_g, sum_b, loss = pl.pallas_call(
        kernel,
        name="crps_head",
        out_shape=(pltpu.VMEM((PTS, H), BF16), pltpu.VMEM((C, H), F32), pltpu.VMEM((1, H), F32), pltpu.VMEM((1, C), F32), pltpu.VMEM((1, 1), F32)),
        in_specs=[hbm, hbm, vmem, vmem, vmem, vmem, smem, vmem],
        out_specs=(vmem,) * 5,
        scratch_shapes=[
            buf(PTS, H, kind=BF16), buf(C, LANES, kind=BF16),
            buf(LANES, H, kind=BF16), buf(LANES, H, kind=BF16),
            buf(LANES, LANES), buf(LANES, LANES), buf(16, LANES), buf(2 * HALF, LANES),
            buf(LANES, LANES),
            buf(PTS, H, kind=BF16), buf(PTS, 1), buf(PTS, 1),
            buf(MEMBERS, HALF, LANES), buf(MEMBERS, HALF, LANES),
            buf(MEMBERS, HALF, LANES), buf(MEMBERS, HALF, LANES),
            buf(2 * HALF, PTS),
            buf(2, NX, PIECES, 16, LANES), buf(NX, PIECES, 16, LANES),
            buf(NX, PIECES, 16, LANES), buf(NX, PIECES, 16, LANES), buf(PIECES, 16, LANES),
            buf(NY, 16, LANES), buf(16, LANES), buf(NZ, 16, LANES), buf(2, NX, PIECES, 16, LANES),
            sems(BLOCKS), pltpu.SemaphoreType.DMA,
            sems(MEMBERS), sems(MEMBERS), sems(MEMBERS), sems(MEMBERS), sems(NX), sems(NX),
            sems(NX), sems(NX), sems(NY), sems(NY), sems(NZ), sems(NZ),
            sems(NY), sems(NX, PIECES), sems(PIECES), sems(NX, PIECES), sems(NX, PIECES), sems(NX, PIECES),
        ],
        compiler_params=pltpu.CompilerParams(collective_id=0, has_side_effects=True),
    )(
        latent.reshape(PTS, H), target[0], weight, bias[None], gain[None], channel_weight[None],
        band_offsets, row_points[None],
    )
    return (grad_x[None, None], sum_w, sum_b[0], sum_g[0], loss[0, 0])


def solution(mesh):
    return jax.shard_map(
        shards,
        mesh=mesh,
        in_specs=(
            P("member", "dp", "space", None),
            P("dp", None, "space"),
            P(), P(), P(), P(), P(), P(),
        ),
        out_specs=(P("member", "dp", "space", None), P(), P(), P(), P()),
        check_vma=False,
    )
```

```python
import jax
import jax.numpy as jnp
from jax import lax
from jax.experimental import pallas as pl
from jax.experimental.pallas import tpu as pltpu
from jax.sharding import PartitionSpec as P

MESH = pl.DeviceIdType.MESH
F32 = jnp.float32
BF16 = jnp.bfloat16
H, C, PTS = 1024, 100, 1024
MEMBERS, NX, NY, NZ, YLO = 16, 4, 8, 8, 4
HALF, REST, FIRST, LANES, BLOCKS, PIECES = 56, 48, 32, 128, 8, 7
SMOOTH = 0.01


def remote(src, dst, send, recv, where):
    return pltpu.make_async_remote_copy(
        src_ref=src, dst_ref=dst, send_sem=send, recv_sem=recv, device_id=where, device_id_type=MESH
    )


def kernel(
    lat_in, tgt, weight, bias, gain, chan, offsets, row_points,
    out_lat, out_w, out_g, out_b, out_loss,
    lat, tbuf,
    wpad, wgain, bcol, qcol, rows, tpad, bsum,
    scaled, s_mean, s_inv, pred, got, back, grads, dlow,
    full, r_core, sum_core, r_x, sum_x, r_y, sum_y, r_z, final,
    l_sem, t_sem, a_send, a_recv, b_send, b_recv, c_send, c_recv, x_send, x_recv, y_send, y_recv,
    z_send, z_recv, gy_send, gx_send, g_recv, gm_send, gm_recv,
):
    me = lax.axis_index("member")
    sp = lax.axis_index("space")
    dp = lax.axis_index("dp")
    my_x, y_lo = me // YLO, me % YLO
    my_y = dp * YLO + y_lo
    my_z, core = sp // 2, sp % 2
    far = (dp + 1) % 2
    mate = my_z * 2 + (1 - core)
    block, half = me // 2, me % 2

    barrier = pltpu.get_barrier_semaphore()

    @pl.loop(1, MEMBERS)
    def _(i):
        pl.semaphore_signal(barrier, inc=1, device_id={"member": (me + i) % MEMBERS}, device_id_type=MESH)

    @pl.loop(0, YLO)
    def _(i):
        pl.semaphore_signal(
            barrier, inc=1, device_id={"member": my_x * YLO + i, "dp": far}, device_id_type=MESH
        )

    @pl.loop(1, NZ)
    def _(i):
        pl.semaphore_signal(
            barrier, inc=1, device_id={"space": ((my_z + i) % NZ) * 2 + core}, device_id_type=MESH
        )

    pl.semaphore_signal(barrier, inc=1, device_id={"space": mate}, device_id_type=MESH)

    def block_at(i):
        return (block + 1 + i) % BLOCKS

    def member_at(i):
        return (me + 1 + i) % MEMBERS

    def seg(ref, k, g, h):
        return ref.at[k, 0:FIRST] if g == 0 else ref.at[k, FIRST : REST if h else HALF]

    def ahead(g, k, slot, h):
        return remote(
            seg(pred, k, g, h), seg(got, slot, g, h), a_send.at[g, k], a_recv.at[g, slot], {"member": k}
        )

    def home(g, k, slot, h):
        return remote(
            seg(back, k, g, h), seg(grads, slot, g, h), b_send.at[g, k], b_recv.at[g, slot], {"member": k}
        )

    def peers(fn):
        @pl.loop(0, MEMBERS - 1)
        def _(i):
            fn(member_at(i))

    def by_half(fn):
        for h in range(2):
            pl.when(half == h)(lambda h=h: fn(h))

    def by_peer(fn):
        for h in range(2):

            @pl.loop(0, BLOCKS)
            def _(i):
                k = (2 * (block + 1 + i) + h) % MEMBERS
                pl.when(k != me)(lambda: fn(k, h))

    def load(i):
        j = block_at(i)
        pts = pl.ds(pl.multiple_of(j * LANES, LANES), LANES)
        return pltpu.make_async_copy(lat_in.at[pts, :], lat.at[pts, :], l_sem.at[j])

    @pl.loop(0, BLOCKS)
    def _(i):
        load(i).start()

    mine = pl.ds(pl.multiple_of(block * LANES, LANES), LANES)
    load_target = pltpu.make_async_copy(tgt.at[:, mine], tbuf, t_sem)
    load_target.start()

    wpad[96:128, :] = jnp.zeros((32, H), BF16)
    wpad[0:C, :] = weight[...]
    rows[...] = jnp.zeros((16, LANES), F32)
    rows[0:1, 0:C] = bias[...]
    rows[8:9, 0:C] = chan[...]
    bcol[...] = jnp.transpose(jnp.broadcast_to(rows[0:1, :], (LANES, LANES)))
    qcol[...] = jnp.transpose(jnp.broadcast_to(rows[8:9, :], (LANES, LANES)))
    pl.semaphore_wait(barrier, (MEMBERS - 1) + YLO + (NZ - 1) + 1)

    @pl.loop(0, BLOCKS)
    def _(i):
        j = block_at(i)
        pts = pl.ds(pl.multiple_of(j * LANES, LANES), LANES)
        load(i).wait()
        values = lat[pts, :].astype(F32)
        mean = jnp.sum(values, axis=1, keepdims=True) * (1.0 / H)
        centered = values - mean
        var = jnp.sum(centered * centered, axis=1, keepdims=True) * (1.0 / H)
        inv = lax.rsqrt(var + 1e-05)
        low = ((centered * inv) * gain[...]).astype(BF16)
        scaled[pts, :] = low
        s_mean[pts, :] = mean
        s_inv[pts, :] = inv
        out = lax.dot_general(
            wpad[0 : 2 * HALF, :], low, (((1,), (1,)), ((), ())), preferred_element_type=F32
        )
        out = out + bcol[0 : 2 * HALF, :]
        for r in range(2):
            k = 2 * j + r
            pred[k] = out[r * HALF : (r + 1) * HALF]

            @pl.when(k != me)
            def _():
                ahead(0, k, me, r).start()

    @pl.loop(0, BLOCKS)
    def _(i):
        for h in range(2):
            k = 2 * block_at(i) + h
            pl.when(k != me)(lambda k=k, h=h: ahead(1, k, me, h).start())

    load_target.wait()
    tpad[96:112, :] = jnp.zeros((16, LANES), F32)
    tpad[0:C, :] = tbuf[...].astype(F32)
    bsum[...] = jnp.zeros((LANES, LANES), F32)
    got[me] = pred[me]

    row_ids = lax.broadcasted_iota(jnp.int32, (1, LANES), 1)
    counts = row_points[...].astype(F32)
    in_band = (row_ids >= offsets[sp]) & (row_ids < offsets[sp + 1])
    live_count = jnp.sum(jnp.where(in_band, counts, 0.0), axis=1, keepdims=True)
    total_live = jnp.sum(jnp.where(row_ids < offsets[16], counts, 0.0), axis=1, keepdims=True)
    live_row = ((row_ids + block * LANES).astype(F32) < live_count).astype(F32)

    wg = wpad[...].astype(F32) * gain[...]
    wgain[...] = (wg - jnp.sum(wg, axis=1, keepdims=True) * (1.0 / H)).astype(BF16)

    peers(lambda k: ahead(0, k, k, 0).wait_recv())

    pair = 1.0 / (MEMBERS - 1)

    def tile(t, score):
        row = pl.multiple_of(t * 8, 8)
        here = pl.ds(row, 8)
        band = pl.ds(pl.multiple_of(half * HALF + row, 8), 8)
        q = qcol[band, :] * live_row
        obs = tpad[band, :]
        p = [got[m, here, :] for m in range(MEMBERS)]
        slope = [None] * MEMBERS
        spread = jnp.zeros((8, LANES), F32)
        for m in range(MEMBERS):
            for n in range(m + 1, MEMBERS):
                gap = p[m] - p[n]
                square = gap * gap + SMOOTH
                root = lax.rsqrt(square)
                spread = spread + square * root
                sign = gap * root
                slope[m] = sign if slope[m] is None else slope[m] + sign
                slope[n] = -sign if slope[n] is None else slope[n] - sign
        skill = jnp.zeros((8, LANES), F32)
        total = jnp.zeros((8, LANES), F32)
        for m in range(MEMBERS):
            gap = p[m] - obs
            square = gap * gap + SMOOTH
            root = lax.rsqrt(square)
            skill = skill + square * root
            sign = gap * root
            total = total + sign
            back[m, here, :] = q * (sign - pair * slope[m])
        bsum[band, :] = q * total
        return score + q * (skill - pair * spread)

    score = lax.fori_loop(0, FIRST // 8, tile, jnp.zeros((8, LANES), F32))
    peers(lambda k: home(0, k, me, 0).start())
    by_half(lambda h: peers(lambda k: ahead(1, k, k, h).wait_recv()))
    score = lax.fori_loop(FIRST // 8, HALF // 8 - half, tile, score)
    by_half(lambda h: peers(lambda k: home(1, k, me, h).start()))
    score = jnp.sum(jnp.sum(score, axis=1, keepdims=True), axis=0, keepdims=True)

    grads[me] = back[me]
    bias_row = jnp.sum(jnp.transpose(bsum[...]), axis=0, keepdims=True)
    row_id = lax.broadcasted_iota(jnp.int32, (16, LANES), 0)
    extra = jnp.where(row_id == 4, bias_row, jnp.where(row_id == 5, score, 0.0))

    by_peer(lambda k, h: home(0, k, k, h).wait_recv())
    by_peer(lambda k, h: home(1, k, k, h).wait_recv())

    dlow[HALF + REST : 2 * HALF, :] = jnp.zeros((HALF - REST, PTS), F32)
    for j in range(BLOCKS):
        pts = slice(j * LANES, (j + 1) * LANES)
        dlow[0:HALF, pts] = grads[2 * j]
        dlow[HALF : HALF + REST, pts] = grads[2 * j + 1, 0:REST]

    dl = dlow[...].astype(BF16)
    for tile_id in range(8):
        gw = jnp.dot(
            dl, scaled[:, tile_id * LANES : (tile_id + 1) * LANES], preferred_element_type=F32
        )
        for g in range(PIECES):
            piece = gw[g * 16 : (g + 1) * 16]
            if tile_id == 0 and g == 6:
                piece = piece + extra
            full[tile_id // 4, tile_id % 4, g] = piece

    def to_mate(x):
        return remote(
            full.at[1 - core, x], r_core.at[x], c_send.at[x], c_recv.at[x], {"space": mate}
        )

    def to_x(k, slot):
        return remote(
            sum_core.at[k], r_x.at[slot], x_send.at[k], x_recv.at[slot], {"member": k * YLO + y_lo}
        )

    @pl.loop(1, NX + 1)
    def _(i):
        to_mate((my_x + i) % NX).start()

    def latent_block(j):
        pts = pl.ds(pl.multiple_of(j * LANES, LANES), LANES)
        d = dlow[:, pts].astype(BF16).astype(F32)
        plain = jnp.concatenate([pred[2 * j], pred[2 * j + 1]], axis=0) - bcol[0 : 2 * HALF, :]
        second = jnp.sum(d * plain, axis=0, keepdims=True) * (1.0 / H)
        second = jnp.transpose(jnp.broadcast_to(second, (LANES, LANES)))[:, 0:1]
        d = jnp.concatenate([d, jnp.zeros((16, LANES), F32)], axis=0)
        dunit = jnp.dot(jnp.transpose(d).astype(BF16), wgain[...], preferred_element_type=F32)
        inv = s_inv[pts, :]
        unit = (lat[pts, :].astype(F32) - s_mean[pts, :]) * inv
        out_lat[pts, :] = (inv * (dunit - unit * second)).astype(BF16)

    pl.loop(0, 1)(latent_block)
    for g in range(2):
        by_peer(lambda k, h: ahead(g, k, k, h).wait_send())
        by_half(lambda h: peers(lambda k: home(g, k, k, h).wait_send()))

    @pl.loop(1, NX)
    def _(i):
        k = (my_x + i) % NX
        to_mate(k).wait()
        sum_core[k] = full[core, k] + r_core[k]
        to_x(k, my_x).start()

    to_mate(my_x).wait()
    r_x[my_x] = full[core, my_x] + r_core[my_x]
    pl.loop(1, 4)(latent_block)

    @pl.loop(1, NX)
    def _(i):
        k = (my_x + i) % NX
        to_x(k, k).wait()

    sum_x[...] = (r_x[0] + r_x[1]) + (r_x[2] + r_x[3])

    def at_y(k):
        return {"member": my_x * YLO + k % YLO, "dp": k // YLO}

    owner = my_y < PIECES

    @pl.loop(1, NY)
    def _(i):
        k = (my_y + i) % NY

        @pl.when(k < PIECES)
        def _():
            remote(sum_x.at[k], r_y.at[my_y], y_send.at[k], y_recv.at[my_y], at_y(k)).start()

    pl.loop(4, 6)(latent_block)

    @pl.loop(1, NY)
    def _(i):
        k = (my_y + i) % NY

        @pl.when(k < PIECES)
        def _():
            remote(sum_x.at[k], r_y.at[my_y], y_send.at[k], y_recv.at[my_y], at_y(k)).wait_send()

        @pl.when(owner)
        def _():
            remote(sum_x.at[0], r_y.at[k], y_send.at[k], y_recv.at[k], at_y(k)).wait_recv()

    @pl.when(owner)
    def _():
        r_y[my_y] = sum_x[my_y]
        sum_y[...] = jnp.sum(r_y[...], axis=0)

        @pl.loop(1, NZ)
        def _(i):
            k = (my_z + i) % NZ
            remote(sum_y, r_z.at[my_z], z_send.at[k], z_recv.at[my_z], {"space": k * 2 + core}).start()

        r_z[my_z] = sum_y[...]

    pl.loop(6, 8)(latent_block)

    def spread_y(k):
        piece = final.at[core, my_x, my_y]
        return remote(piece, piece, gy_send.at[k], g_recv.at[my_x, my_y], at_y(k))

    def spread_x(k, x):
        piece = final.at[core, my_x, k]
        return remote(
            piece, piece, gx_send.at[x, k], g_recv.at[my_x, k], {"member": x * YLO + y_lo}
        )

    def arrived(x, k):
        piece = final.at[core, x, k]
        return remote(piece, piece, gy_send.at[0], g_recv.at[x, k], {"space": mate})

    def spread_mate(x, k):
        piece = final.at[core, x, k]
        return remote(piece, piece, gm_send.at[x, k], gm_recv.at[x, k], {"space": mate})

    def mate_arrived(x, k):
        piece = final.at[1 - core, x, k]
        return remote(piece, piece, gm_send.at[x, k], gm_recv.at[x, k], {"space": mate})

    @pl.when(owner)
    def _():
        @pl.loop(1, NZ)
        def _(i):
            k = (my_z + i) % NZ
            remote(sum_y, r_z.at[k], z_send.at[k], z_recv.at[k], {"space": k * 2 + core}).wait()

        final[core, my_x, my_y] = jnp.sum(r_z[...], axis=0)

        @pl.loop(1, NY)
        def _(i):
            spread_y((my_y + i) % NY).start()

    @pl.loop(0, NY)
    def _(i):
        k = (my_y + i) % NY

        @pl.when(k < PIECES)
        def _():
            @pl.when(i > 0)
            def _():
                arrived(my_x, k).wait_recv()

            @pl.loop(1, NX)
            def _(d):
                spread_x(k, (my_x + d) % NX).start()

            spread_mate(my_x, k).start()

    @pl.loop(0, NY)
    def _(i):
        k = (my_y + i) % NY

        @pl.when(k < PIECES)
        def _():
            @pl.loop(1, NX)
            def _(d):
                x = (my_x + d) % NX
                arrived(x, k).wait_recv()
                spread_mate(x, k).start()

    @pl.when(owner)
    def _():
        @pl.loop(1, NY)
        def _(i):
            spread_y((my_y + i) % NY).wait_send()

    @pl.loop(0, PIECES)
    def _(k):
        @pl.loop(1, NX)
        def _(d):
            spread_x(k, (my_x + d) % NX).wait_send()

        @pl.loop(0, NX)
        def _(x):
            spread_mate(x, k).wait_send()
            mate_arrived(x, k).wait_recv()

    for tile_id in range(8):
        cols = slice(tile_id * LANES, (tile_id + 1) * LANES)
        acc = jnp.zeros((16, LANES), F32)
        for g in range(PIECES):
            piece = final[tile_id // 4, tile_id % 4, g]
            top = min(16, C - g * 16)
            out_w[g * 16 : g * 16 + top, cols] = piece[0:top]
            acc = acc + piece * wpad[g * 16 : (g + 1) * 16, cols].astype(F32)
        out_g[0:1, cols] = jnp.sum(acc, axis=0, keepdims=True) / gain[0:1, cols]
    out_b[...] = final[0, 0, 6, 4:5, 0:C]
    out_loss[...] = final[0, 0, 6, 5:6, 0:1] / (C * 2.0 * total_live)


def shards(latent, target, weight, bias, gain, channel_weight, band_offsets, row_points):
    vmem = pl.BlockSpec(memory_space=pltpu.VMEM)

    def buf(*shape, kind=F32):
        return pltpu.VMEM(shape, kind)

    def sems(*shape):
        return pltpu.SemaphoreType.DMA(shape)

    hbm = pl.BlockSpec(memory_space=pl.ANY)
    smem = pl.BlockSpec(memory_space=pltpu.SMEM)
    grad_x, sum_w, sum_g, sum_b, loss = pl.pallas_call(
        kernel,
        name="crps_head",
        out_shape=(pltpu.VMEM((PTS, H), BF16), pltpu.VMEM((C, H), F32), pltpu.VMEM((1, H), F32), pltpu.VMEM((1, C), F32), pltpu.VMEM((1, 1), F32)),
        in_specs=[hbm, hbm, vmem, vmem, vmem, vmem, smem, vmem],
        out_specs=(vmem,) * 5,
        scratch_shapes=[
            buf(PTS, H, kind=BF16), buf(C, LANES, kind=BF16),
            buf(LANES, H, kind=BF16), buf(LANES, H, kind=BF16),
            buf(LANES, LANES), buf(LANES, LANES), buf(16, LANES), buf(2 * HALF, LANES),
            buf(LANES, LANES),
            buf(PTS, H, kind=BF16), buf(PTS, 1), buf(PTS, 1),
            buf(MEMBERS, HALF, LANES), buf(MEMBERS, HALF, LANES),
            buf(MEMBERS, HALF, LANES), buf(MEMBERS, HALF, LANES),
            buf(2 * HALF, PTS),
            buf(2, NX, PIECES, 16, LANES), buf(NX, PIECES, 16, LANES),
            buf(NX, PIECES, 16, LANES), buf(NX, PIECES, 16, LANES), buf(PIECES, 16, LANES),
            buf(NY, 16, LANES), buf(16, LANES), buf(NZ, 16, LANES), buf(2, NX, PIECES, 16, LANES),
            sems(BLOCKS), pltpu.SemaphoreType.DMA,
            sems(2, MEMBERS), sems(2, MEMBERS), sems(2, MEMBERS), sems(2, MEMBERS), sems(NX), sems(NX),
            sems(NX), sems(NX), sems(NY), sems(NY), sems(NZ), sems(NZ),
            sems(NY), sems(NX, PIECES), sems(NX, PIECES), sems(NX, PIECES), sems(NX, PIECES),
        ],
        compiler_params=pltpu.CompilerParams(collective_id=0, has_side_effects=True),
    )(
        latent.reshape(PTS, H), target[0], weight, bias[None], gain[None], channel_weight[None],
        band_offsets, row_points[None],
    )
    return (grad_x[None, None], sum_w, sum_b[0], sum_g[0], loss[0, 0])


def solution(mesh):
    return jax.shard_map(
        shards,
        mesh=mesh,
        in_specs=(
            P("member", "dp", "space", None),
            P("dp", None, "space"),
            P(), P(), P(), P(), P(), P(),
        ),
        out_specs=(P("member", "dp", "space", None), P(), P(), P(), P()),
        check_vma=False,
    )
```

```python
import jax
import jax.numpy as jnp
from jax import lax
from jax.experimental import pallas as pl
from jax.experimental.pallas import tpu as pltpu
from jax.sharding import PartitionSpec as P

MESH = pl.DeviceIdType.MESH
F32 = jnp.float32
BF16 = jnp.bfloat16
H, C, PTS = 1024, 100, 1024
MEMBERS, NX, NY, NZ, YLO = 16, 4, 8, 8, 4
HALF, REST, FIRST, LANES, BLOCKS, PIECES = 56, 48, 32, 128, 8, 7
SMOOTH = 0.01


def remote(src, dst, send, recv, where):
    return pltpu.make_async_remote_copy(
        src_ref=src, dst_ref=dst, send_sem=send, recv_sem=recv, device_id=where, device_id_type=MESH
    )


def kernel(
    lat_in, tgt, weight, bias, gain, chan, offsets, row_points,
    out_lat, out_w, out_g, out_b, out_loss,
    lat, tbuf,
    wpad, wgain, bcol, qcol, rows, tpad, bsum,
    scaled, s_mean, s_inv, pred, got, back, grads, dlow,
    full, r_core, sum_core, r_x, sum_x, r_y, sum_y, r_z, final,
    l_sem, t_sem, a_send, a_recv, b_send, b_recv, c_send, c_recv, x_send, x_recv, y_send, y_recv,
    z_send, z_recv, gy_send, gx_send, g_recv, gm_send, gm_recv,
):
    me = lax.axis_index("member")
    sp = lax.axis_index("space")
    dp = lax.axis_index("dp")
    my_x, y_lo = me // YLO, me % YLO
    my_y = dp * YLO + y_lo
    my_z, core = sp // 2, sp % 2
    far = (dp + 1) % 2
    mate = my_z * 2 + (1 - core)
    block, half = me // 2, me % 2

    barrier = pltpu.get_barrier_semaphore()

    @pl.loop(1, MEMBERS)
    def _(i):
        pl.semaphore_signal(barrier, inc=1, device_id={"member": (me + i) % MEMBERS}, device_id_type=MESH)

    @pl.loop(0, YLO)
    def _(i):
        pl.semaphore_signal(
            barrier, inc=1, device_id={"member": my_x * YLO + i, "dp": far}, device_id_type=MESH
        )

    @pl.loop(1, NZ)
    def _(i):
        pl.semaphore_signal(
            barrier, inc=1, device_id={"space": ((my_z + i) % NZ) * 2 + core}, device_id_type=MESH
        )

    pl.semaphore_signal(barrier, inc=1, device_id={"space": mate}, device_id_type=MESH)

    def block_at(i):
        return (block + 1 + i) % BLOCKS

    def member_at(i):
        return (me + 1 + i) % MEMBERS

    def seg(ref, k, g, h):
        return ref.at[k, 0:FIRST] if g == 0 else ref.at[k, FIRST : REST if h else HALF]

    def ahead(g, k, slot, h):
        return remote(
            seg(pred, k, g, h), seg(got, slot, g, h), a_send.at[g, k], a_recv.at[g, slot], {"member": k}
        )

    def home(g, k, slot, h):
        return remote(
            seg(back, k, g, h), seg(grads, slot, g, h), b_send.at[g, k], b_recv.at[g, slot], {"member": k}
        )

    def peers(fn):
        @pl.loop(0, MEMBERS - 1)
        def _(i):
            fn(member_at(i))

    def by_half(fn):
        for h in range(2):
            pl.when(half == h)(lambda h=h: fn(h))

    def by_peer(fn):
        for h in range(2):

            @pl.loop(0, BLOCKS)
            def _(i):
                k = (2 * (block + 1 + i) + h) % MEMBERS
                pl.when(k != me)(lambda: fn(k, h))

    def load(i):
        j = block_at(i)
        pts = pl.ds(pl.multiple_of(j * LANES, LANES), LANES)
        return pltpu.make_async_copy(lat_in.at[pts, :], lat.at[pts, :], l_sem.at[j])

    @pl.loop(0, BLOCKS)
    def _(i):
        load(i).start()

    mine = pl.ds(pl.multiple_of(block * LANES, LANES), LANES)
    load_target = pltpu.make_async_copy(tgt.at[:, mine], tbuf, t_sem)
    load_target.start()

    wpad[96:128, :] = jnp.zeros((32, H), BF16)
    wpad[0:C, :] = weight[...]
    rows[...] = jnp.zeros((16, LANES), F32)
    rows[0:1, 0:C] = bias[...]
    rows[8:9, 0:C] = chan[...]
    bcol[...] = jnp.transpose(jnp.broadcast_to(rows[0:1, :], (LANES, LANES)))
    qcol[...] = jnp.transpose(jnp.broadcast_to(rows[8:9, :], (LANES, LANES)))
    pl.semaphore_wait(barrier, (MEMBERS - 1) + YLO + (NZ - 1) + 1)

    @pl.loop(0, BLOCKS)
    def _(i):
        j = block_at(i)
        pts = pl.ds(pl.multiple_of(j * LANES, LANES), LANES)
        load(i).wait()
        values = lat[pts, :].astype(F32)
        mean = jnp.sum(values, axis=1, keepdims=True) * (1.0 / H)
        centered = values - mean
        var = jnp.sum(centered * centered, axis=1, keepdims=True) * (1.0 / H)
        inv = lax.rsqrt(var + 1e-05)
        low = ((centered * inv) * gain[...]).astype(BF16)
        scaled[pts, :] = low
        s_mean[pts, :] = mean
        s_inv[pts, :] = inv
        out = lax.dot_general(
            wpad[0 : 2 * HALF, :], low, (((1,), (1,)), ((), ())), preferred_element_type=F32
        )
        out = out + bcol[0 : 2 * HALF, :]
        for r in range(2):
            k = 2 * j + r
            pred[k] = out[r * HALF : (r + 1) * HALF]

            @pl.when(k != me)
            def _():
                ahead(0, k, me, r).start()

    @pl.loop(0, BLOCKS)
    def _(i):
        for h in range(2):
            k = 2 * block_at(i) + h
            pl.when(k != me)(lambda k=k, h=h: ahead(1, k, me, h).start())

    load_target.wait()
    tpad[96:112, :] = jnp.zeros((16, LANES), F32)
    tpad[0:C, :] = tbuf[...].astype(F32)
    bsum[...] = jnp.zeros((LANES, LANES), F32)
    got[me] = pred[me]

    row_ids = lax.broadcasted_iota(jnp.int32, (1, LANES), 1)
    counts = row_points[...].astype(F32)
    in_band = (row_ids >= offsets[sp]) & (row_ids < offsets[sp + 1])
    live_count = jnp.sum(jnp.where(in_band, counts, 0.0), axis=1, keepdims=True)
    total_live = jnp.sum(jnp.where(row_ids < offsets[16], counts, 0.0), axis=1, keepdims=True)
    live_row = ((row_ids + block * LANES).astype(F32) < live_count).astype(F32)

    wg = wpad[...].astype(F32) * gain[...]
    wgain[...] = (wg - jnp.sum(wg, axis=1, keepdims=True) * (1.0 / H)).astype(BF16)

    peers(lambda k: ahead(0, k, k, 0).wait_recv())

    pair = 1.0 / (MEMBERS - 1)

    def tile(t, score):
        row = pl.multiple_of(t * 8, 8)
        here = pl.ds(row, 8)
        band = pl.ds(pl.multiple_of(half * HALF + row, 8), 8)
        q = qcol[band, :] * live_row
        obs = tpad[band, :]
        p = [got[m, here, :] for m in range(MEMBERS)]
        slope = [None] * MEMBERS
        spread = jnp.zeros((8, LANES), F32)
        for m in range(MEMBERS):
            for n in range(m + 1, MEMBERS):
                gap = p[m] - p[n]
                square = gap * gap + SMOOTH
                root = lax.rsqrt(square)
                spread = spread + square * root
                sign = gap * root
                slope[m] = sign if slope[m] is None else slope[m] + sign
                slope[n] = -sign if slope[n] is None else slope[n] - sign
        skill = jnp.zeros((8, LANES), F32)
        total = jnp.zeros((8, LANES), F32)
        for m in range(MEMBERS):
            gap = p[m] - obs
            square = gap * gap + SMOOTH
            root = lax.rsqrt(square)
            skill = skill + square * root
            sign = gap * root
            total = total + sign
            back[m, here, :] = q * (sign - pair * slope[m])
        bsum[band, :] = q * total
        return score + q * (skill - pair * spread)

    score = lax.fori_loop(0, FIRST // 8, tile, jnp.zeros((8, LANES), F32))
    peers(lambda k: home(0, k, me, 0).start())
    by_half(lambda h: peers(lambda k: ahead(1, k, k, h).wait_recv()))
    score = lax.fori_loop(FIRST // 8, HALF // 8 - half, tile, score)
    by_half(lambda h: peers(lambda k: home(1, k, me, h).start()))
    score = jnp.sum(jnp.sum(score, axis=1, keepdims=True), axis=0, keepdims=True)

    grads[me] = back[me]
    bias_row = jnp.sum(jnp.transpose(bsum[...]), axis=0, keepdims=True)
    row_id = lax.broadcasted_iota(jnp.int32, (16, LANES), 0)
    extra = jnp.where(row_id == 4, bias_row, jnp.where(row_id == 5, score, 0.0))

    by_peer(lambda k, h: home(0, k, k, h).wait_recv())
    by_peer(lambda k, h: home(1, k, k, h).wait_recv())

    dlow[HALF + REST : 2 * HALF, :] = jnp.zeros((HALF - REST, PTS), F32)
    for j in range(BLOCKS):
        pts = slice(j * LANES, (j + 1) * LANES)
        dlow[0:HALF, pts] = grads[2 * j]
        dlow[HALF : HALF + REST, pts] = grads[2 * j + 1, 0:REST]

    dl = dlow[...].astype(BF16)
    for tile_id in range(8):
        gw = jnp.dot(
            dl, scaled[:, tile_id * LANES : (tile_id + 1) * LANES], preferred_element_type=F32
        )
        for g in range(PIECES):
            piece = gw[g * 16 : (g + 1) * 16]
            if tile_id == 0 and g == 6:
                piece = piece + extra
            full[tile_id // 4, tile_id % 4, g] = piece

    def to_mate(x):
        return remote(
            full.at[1 - core, x], r_core.at[x], c_send.at[x], c_recv.at[x], {"space": mate}
        )

    def to_x(k, slot):
        return remote(
            sum_core.at[k], r_x.at[slot], x_send.at[k], x_recv.at[slot], {"member": k * YLO + y_lo}
        )

    @pl.loop(1, NX + 1)
    def _(i):
        to_mate((my_x + i) % NX).start()

    def latent_block(j):
        pts = pl.ds(pl.multiple_of(j * LANES, LANES), LANES)
        d = dlow[:, pts].astype(BF16).astype(F32)
        plain = jnp.concatenate([pred[2 * j], pred[2 * j + 1]], axis=0) - bcol[0 : 2 * HALF, :]
        second = jnp.sum(d * plain, axis=0, keepdims=True) * (1.0 / H)
        second = jnp.transpose(jnp.broadcast_to(second, (LANES, LANES)))[:, 0:1]
        d = jnp.concatenate([d, jnp.zeros((16, LANES), F32)], axis=0)
        dunit = jnp.dot(jnp.transpose(d).astype(BF16), wgain[...], preferred_element_type=F32)
        inv = s_inv[pts, :]
        unit = (lat[pts, :].astype(F32) - s_mean[pts, :]) * inv
        out_lat[pts, :] = (inv * (dunit - unit * second)).astype(BF16)

    pl.loop(0, 1)(latent_block)
    for g in range(2):
        by_peer(lambda k, h: ahead(g, k, k, h).wait_send())
        by_half(lambda h: peers(lambda k: home(g, k, k, h).wait_send()))

    @pl.loop(1, NX)
    def _(i):
        k = (my_x + i) % NX
        to_mate(k).wait()
        sum_core[k] = full[core, k] + r_core[k]
        to_x(k, my_x).start()

    to_mate(my_x).wait()
    r_x[my_x] = full[core, my_x] + r_core[my_x]
    pl.loop(1, 4)(latent_block)

    @pl.loop(1, NX)
    def _(i):
        k = (my_x + i) % NX
        to_x(k, k).wait()

    sum_x[...] = (r_x[0] + r_x[1]) + (r_x[2] + r_x[3])

    def at_y(k):
        return {"member": my_x * YLO + k % YLO, "dp": k // YLO}

    owner = my_y < PIECES

    @pl.loop(1, NY)
    def _(i):
        k = (my_y + i) % NY

        @pl.when(k < PIECES)
        def _():
            remote(sum_x.at[k], r_y.at[my_y], y_send.at[k], y_recv.at[my_y], at_y(k)).start()

    pl.loop(4, 6)(latent_block)

    @pl.loop(1, NY)
    def _(i):
        k = (my_y + i) % NY

        @pl.when(k < PIECES)
        def _():
            remote(sum_x.at[k], r_y.at[my_y], y_send.at[k], y_recv.at[my_y], at_y(k)).wait_send()

        @pl.when(owner)
        def _():
            remote(sum_x.at[0], r_y.at[k], y_send.at[k], y_recv.at[k], at_y(k)).wait_recv()

    @pl.when(owner)
    def _():
        r_y[my_y] = sum_x[my_y]
        sum_y[...] = jnp.sum(r_y[...], axis=0)

        @pl.loop(1, NZ)
        def _(i):
            k = (my_z + i) % NZ
            remote(sum_y, r_z.at[my_z], z_send.at[k], z_recv.at[my_z], {"space": k * 2 + core}).start()

        r_z[my_z] = sum_y[...]

    pl.loop(6, 8)(latent_block)

    def nearest(i):
        step = (i + 1) // 2
        return (my_y + (i % 2) * step + (1 - i % 2) * (NY - step)) % NY

    def spread_y(k):
        piece = final.at[core, my_x, my_y]
        return remote(piece, piece, gy_send.at[k], g_recv.at[my_x, my_y], at_y(k))

    def spread_x(k, x):
        piece = final.at[core, my_x, k]
        return remote(
            piece, piece, gx_send.at[x, k], g_recv.at[my_x, k], {"member": x * YLO + y_lo}
        )

    def arrived(x, k):
        piece = final.at[core, x, k]
        return remote(piece, piece, gy_send.at[0], g_recv.at[x, k], {"space": mate})

    def spread_mate(x, k):
        piece = final.at[core, x, k]
        return remote(piece, piece, gm_send.at[x, k], gm_recv.at[x, k], {"space": mate})

    def mate_arrived(x, k):
        piece = final.at[1 - core, x, k]
        return remote(piece, piece, gm_send.at[x, k], gm_recv.at[x, k], {"space": mate})

    @pl.when(owner)
    def _():
        @pl.loop(1, NZ)
        def _(i):
            k = (my_z + i) % NZ
            remote(sum_y, r_z.at[k], z_send.at[k], z_recv.at[k], {"space": k * 2 + core}).wait()

        final[core, my_x, my_y] = jnp.sum(r_z[...], axis=0)

        @pl.loop(1, NY)
        def _(i):
            spread_y((my_y + i) % NY).start()

    @pl.loop(0, NY)
    def _(i):
        k = nearest(i)

        @pl.when(k < PIECES)
        def _():
            @pl.when(i > 0)
            def _():
                arrived(my_x, k).wait_recv()

            @pl.loop(1, NX)
            def _(d):
                spread_x(k, (my_x + d) % NX).start()

            spread_mate(my_x, k).start()

    @pl.loop(0, NY)
    def _(i):
        k = nearest(i)

        @pl.when(k < PIECES)
        def _():
            @pl.loop(1, NX)
            def _(d):
                x = (my_x + d) % NX
                arrived(x, k).wait_recv()
                spread_mate(x, k).start()

    @pl.when(owner)
    def _():
        @pl.loop(1, NY)
        def _(i):
            spread_y((my_y + i) % NY).wait_send()

    @pl.loop(0, PIECES)
    def _(k):
        @pl.loop(1, NX)
        def _(d):
            spread_x(k, (my_x + d) % NX).wait_send()

        @pl.loop(0, NX)
        def _(x):
            spread_mate(x, k).wait_send()
            mate_arrived(x, k).wait_recv()

    for tile_id in range(8):
        cols = slice(tile_id * LANES, (tile_id + 1) * LANES)
        acc = jnp.zeros((16, LANES), F32)
        for g in range(PIECES):
            piece = final[tile_id // 4, tile_id % 4, g]
            top = min(16, C - g * 16)
            out_w[g * 16 : g * 16 + top, cols] = piece[0:top]
            acc = acc + piece * wpad[g * 16 : (g + 1) * 16, cols].astype(F32)
        out_g[0:1, cols] = jnp.sum(acc, axis=0, keepdims=True) / gain[0:1, cols]
    out_b[...] = final[0, 0, 6, 4:5, 0:C]
    out_loss[...] = final[0, 0, 6, 5:6, 0:1] / (C * 2.0 * total_live)


def shards(latent, target, weight, bias, gain, channel_weight, band_offsets, row_points):
    vmem = pl.BlockSpec(memory_space=pltpu.VMEM)

    def buf(*shape, kind=F32):
        return pltpu.VMEM(shape, kind)

    def sems(*shape):
        return pltpu.SemaphoreType.DMA(shape)

    hbm = pl.BlockSpec(memory_space=pl.ANY)
    smem = pl.BlockSpec(memory_space=pltpu.SMEM)
    grad_x, sum_w, sum_g, sum_b, loss = pl.pallas_call(
        kernel,
        name="crps_head",
        out_shape=(pltpu.VMEM((PTS, H), BF16), pltpu.VMEM((C, H), F32), pltpu.VMEM((1, H), F32), pltpu.VMEM((1, C), F32), pltpu.VMEM((1, 1), F32)),
        in_specs=[hbm, hbm, vmem, vmem, vmem, vmem, smem, vmem],
        out_specs=(vmem,) * 5,
        scratch_shapes=[
            buf(PTS, H, kind=BF16), buf(C, LANES, kind=BF16),
            buf(LANES, H, kind=BF16), buf(LANES, H, kind=BF16),
            buf(LANES, LANES), buf(LANES, LANES), buf(16, LANES), buf(2 * HALF, LANES),
            buf(LANES, LANES),
            buf(PTS, H, kind=BF16), buf(PTS, 1), buf(PTS, 1),
            buf(MEMBERS, HALF, LANES), buf(MEMBERS, HALF, LANES),
            buf(MEMBERS, HALF, LANES), buf(MEMBERS, HALF, LANES),
            buf(2 * HALF, PTS),
            buf(2, NX, PIECES, 16, LANES), buf(NX, PIECES, 16, LANES),
            buf(NX, PIECES, 16, LANES), buf(NX, PIECES, 16, LANES), buf(PIECES, 16, LANES),
            buf(NY, 16, LANES), buf(16, LANES), buf(NZ, 16, LANES), buf(2, NX, PIECES, 16, LANES),
            sems(BLOCKS), pltpu.SemaphoreType.DMA,
            sems(2, MEMBERS), sems(2, MEMBERS), sems(2, MEMBERS), sems(2, MEMBERS), sems(NX), sems(NX),
            sems(NX), sems(NX), sems(NY), sems(NY), sems(NZ), sems(NZ),
            sems(NY), sems(NX, PIECES), sems(NX, PIECES), sems(NX, PIECES), sems(NX, PIECES),
        ],
        compiler_params=pltpu.CompilerParams(collective_id=0, has_side_effects=True),
    )(
        latent.reshape(PTS, H), target[0], weight, bias[None], gain[None], channel_weight[None],
        band_offsets, row_points[None],
    )
    return (grad_x[None, None], sum_w, sum_b[0], sum_g[0], loss[0, 0])


def solution(mesh):
    return jax.shard_map(
        shards,
        mesh=mesh,
        in_specs=(
            P("member", "dp", "space", None),
            P("dp", None, "space"),
            P(), P(), P(), P(), P(), P(),
        ),
        out_specs=(P("member", "dp", "space", None), P(), P(), P(), P()),
        check_vma=False,
    )
```
